768 devices in a mesh: fsdp: 192 (over x, z, y_lo, core), island: 4 (over y_hi).
Axes of the slice: x: 4, y: 8 (y_hi: 4, y_lo: 2; y = y_hi * 2 + y_lo), z: 12, core: 2. Of those that a mesh axis runs over, the one named last changes fastest.
Arguments:
- activations: bfloat16 [4, 24576, 4224], P('island', 'fsdp'), may hold values from -24 to 24
- out_grads: bfloat16 [4, 24576, 512], P('island', 'fsdp'), may hold values from -0.038085938 to 0.038085938
- projection: bfloat16 [4224, 256], P('fsdp'), may hold values from -0.09375 to 0.09375
- first_moment: float32 [4, 1, 256, 512], P('island'), may hold values from -1.8 to 1.8
- second_moment: float32 [4, 1, 256, 512], P('island'), may hold values from 0.01 to 1
- inner_weights: float32 [4, 4224, 512], P('island', 'fsdp'), may hold values from -6 to 6
- global_weights: float32 [4224, 512], P('fsdp'), may hold values from -6 to 6
- outer_momentum: float32 [4224, 512], P('fsdp'), may hold values from -6 to 6
Outputs:
- new_weights: bfloat16 [4224, 512], P('fsdp', 'island')
- new_momentum: float32 [4224, 512], P('fsdp')
- new_first: float32 [4, 1, 256, 512], P('island')
- new_second: float32 [4, 1, 256, 512], P('island')
The draws below stay inside these ranges and needn't reach their ends.
All inputs are finite; a program needn't handle non-finite values.
Results may differ from the reference program's by a relative error of at most 0.001.
Values sent between devices are 32-bit elements; how exact they have to be, the bound alone decides.
A program may use at most 64 MiB of HBM per device.

```python
import math
import jax
import jax.numpy as jnp
from jax import lax

DW = 4224
COLS = 512
RANK = 256
LAYERS = 1
TOKENS = 24576
ROWS = 4224
N_ISLAND = 4


def raised(values, stream_key, source, target, shards_of, factor):
    def block_of(dim):
        return (jnp.arange(values.shape[dim]) // (values.shape[dim] // shards_of)).reshape((-1,) + (1,) * (values.ndim - 1 - dim))

    one_side = jax.random.permutation(stream_key, shards_of)[block_of(target)]
    other_side = (block_of(target) + shards_of // 2) % shards_of
    return jnp.where((block_of(source) == one_side) | (block_of(source) == other_side), factor * values, values)


def block_scale(own_key, extent, cuts, smallest, largest):
    level, own = 1.0, jax.random.fold_in(own_key, 6)
    for axis_at, parts in cuts:
        steps = jnp.exp(jax.random.uniform(jax.random.fold_in(own, axis_at), (parts,), jnp.float32, smallest / len(cuts), largest / len(cuts)))
        level = level * jnp.repeat(steps, extent[axis_at] // parts).reshape([-1 if axis == axis_at else 1 for axis in range(len(extent))])
    return level


def bell_draw(rng, shape, width, most, shards=(), kind=jnp.bfloat16):
    drawn = width * jax.random.normal(rng, shape, jnp.float32)
    if shards:
        drawn = drawn * block_scale(rng, shape, shards, -0.22, 0.18)
    return jnp.clip(drawn, -most, most).astype(kind)


def gaussian_with(rng, shape, spread, limit, cuts, heavy, kind=jnp.bfloat16):
    drawn = spread * jax.random.normal(rng, shape, jnp.float32)
    if cuts:
        drawn = drawn * block_scale(rng, shape, cuts, -0.22, 0.18)
    return jnp.clip(raised(drawn, jax.random.fold_in(rng, 3), *heavy), -limit, limit).astype(kind)


def setup_inputs(seed: int = 0) -> dict:
    arg_keys = jax.random.split(jax.random.key(seed), 9)
    activations = gaussian_with(arg_keys[0], (N_ISLAND, TOKENS, ROWS), 1.0, 24.0, ((0, 4), (1, 192)), (1, 2, 192, 6.0))
    out_grads = bell_draw(arg_keys[1], (N_ISLAND, TOKENS, LAYERS * COLS), (TOKENS ** -0.5), 0.038085938, ((0, 4), (1, 192)))
    projection = bell_draw(arg_keys[2], (ROWS, RANK), DW ** -0.5, 0.09375, ((0, 192),))
    first_moment = bell_draw(arg_keys[3], (N_ISLAND, LAYERS, RANK, COLS), 0.3, 1.8, ((0, 4),), jnp.float32)
    second_moment = jnp.clip(jnp.exp(math.log(1.0) - 4.6051702 * jax.random.uniform(arg_keys[4], (N_ISLAND, LAYERS, RANK, COLS), jnp.float32) ** block_scale(arg_keys[4], (N_ISLAND, LAYERS, RANK, COLS), ((0, 4),), -0.2, 0.2)), 0.01, 1.0)
    inner_weights = bell_draw(arg_keys[5], (N_ISLAND, ROWS, COLS), 1.0, 6.0, ((0, 4), (1, 192)), jnp.float32)
    global_weights = bell_draw(arg_keys[6], (ROWS, COLS), 1.0, 6.0, ((0, 192),), jnp.float32)
    outer_momentum = bell_draw(arg_keys[7], (ROWS, COLS), 1.0, 6.0, ((0, 192),), jnp.float32)
    return {"activations": activations, "out_grads": out_grads, "projection": projection, "first_moment": first_moment, "second_moment": second_moment, "inner_weights": inner_weights, "global_weights": global_weights, "outer_momentum": outer_momentum}


first_decay = 0.9
second_decay = 0.999
first_fix = 1.0 - 0.9 ** 10
second_fix = 1.0 - 0.999 ** 10
epsilon = 1e-08
inner_rate = 1.0
outer_rate = 0.7
outer_beta = 0.9

def reference(activations, out_grads, projection, first_moment, second_moment, inner_weights, global_weights, outer_momentum):
    stepped_list = []
    first_list = []
    second_list = []
    for island_index in range(N_ISLAND):
        inputs = activations[island_index]
        grads_out = out_grads[island_index]
        pieces = []
        projected_list = []
        for layer_index in range(LAYERS):
            block = inputs[:, layer_index * DW:(layer_index + 1) * DW]
            grad_block = grads_out[:, layer_index * COLS:(layer_index + 1) * COLS]
            gradient = jnp.dot(block.T, grad_block, preferred_element_type=jnp.float32)
            pieces.append(gradient)
            proj_block = projection[layer_index * DW:(layer_index + 1) * DW].astype(jnp.float32)
            projected_list.append(jnp.dot(proj_block.T, gradient, precision=lax.Precision.HIGHEST))
        gradient_all = jnp.concatenate(pieces, axis=0)
        projected = jnp.stack(projected_list)
        new_first = first_decay * first_moment[island_index] + (1.0 - first_decay) * projected
        new_second = second_decay * second_moment[island_index] + (1.0 - second_decay) * projected * projected
        adapted = new_first / first_fix / (jnp.sqrt(new_second / second_fix) + epsilon)
        channel_scale = jnp.sqrt(lax.optimization_barrier(jnp.mean(adapted * adapted, axis=1))) / jnp.sqrt(lax.optimization_barrier(jnp.mean(projected * projected, axis=1)) + 1e-06)
        row_scale = jnp.repeat(channel_scale, DW, axis=0)
        stepped_list.append(inner_weights[island_index] - inner_rate * gradient_all * row_scale)
        first_list.append(new_first)
        second_list.append(new_second)
    island_total = stepped_list[0]
    for island_index in range(1, N_ISLAND):
        island_total = island_total + stepped_list[island_index]
    pseudo_grad = global_weights - island_total / N_ISLAND
    new_momentum = outer_beta * outer_momentum + pseudo_grad
    new_weights = (global_weights - outer_rate * (pseudo_grad + outer_beta * new_momentum)).astype(jnp.bfloat16)
    return (new_weights, new_momentum, jnp.stack(first_list), jnp.stack(second_list))
```

```python
import functools

import jax
import jax.numpy as jnp
from jax import lax
from jax.experimental import pallas as pl
from jax.experimental.pallas import tpu as pltpu
from jax.sharding import Mesh
from jax.sharding import PartitionSpec as P

RANK = 256
X, Z, Y, C = "fsdp_0", "fsdp_1", "fsdp_2", "fsdp_3"
ISLAND = "island"
FSDP = (X, Z, Y, C)
LANES = 128
MESH_ID = pl.DeviceIdType.MESH
F32 = jnp.float32

first_decay = 0.9
second_decay = 0.999
first_fix = 1.0 - 0.9**10
second_fix = 1.0 - 0.999**10
epsilon = 1e-08
inner_rate = 1.0
outer_rate = 0.7
outer_beta = 0.9


class Lanes:
    def __init__(self, send_sems, recv_sems):
        self.send_sems, self.recv_sems = send_sems, recv_sems
        self.used = 0
        self.started = []

    def send(self, src, dst, **peer):
        copy = pltpu.make_async_remote_copy(
            src_ref=src,
            dst_ref=dst,
            send_sem=self.send_sems.at[self.used],
            recv_sem=self.recv_sems.at[self.used],
            device_id=peer,
            device_id_type=MESH_ID,
        )
        self.used += 1
        copy.start()
        self.started.append(copy)
        return copy


def turn(axis, by):
    size = lax.axis_size(axis)
    return lax.rem(lax.axis_index(axis) + by + size, size)


def chain(lanes, axis, steps, way, block, slots):
    copy = None
    for step in range(steps):
        at = block(turn(axis, way * (steps - step)))
        if copy is not None:
            copy.wait_recv()
            at[...] = at[...] + slots[step - 1]
        copy = lanes.send(at, slots.at[step], **{axis: turn(axis, way)})
        yield
    copy.wait_recv()
    at = block(lax.axis_index(axis))
    at[...] = at[...] + slots[steps - 1]


def advance(chains):
    for one in chains:
        next(one, None)


def comm_kernel(
    a_ref, g_ref, p_ref, first_ref, second_ref, w_ref,
    proj_ref, total_ref,
    a_out, a_in, g_out, g_in, p_out, p_in, p_all,
    part_z, part_x,
    z_up, z_down, x_up, x_down, zx_up, zx_down, xz_up, xz_down,
    y_z, y_x, grad, grad_own, w_all, grad_all,
    proj_part, proj_x, proj_z, proj_all, stats, scales, scale_all,
    send_sems, recv_sems,
):
    xk, zk, yk, ck = (lax.axis_index(name) for name in FSDP)
    island = lax.axis_index(ISLAND)
    nx, nz = lax.axis_size(X), lax.axis_size(Z)
    ni = lax.axis_size(ISLAND)
    lanes = Lanes(send_sems, recv_sems)
    other_c, other_y = 1 - ck, 1 - yk
    quad = yk * 2 + ck
    half = g_ref.shape[1] // 2
    rows = p_ref.shape[0]
    mine = pl.ds(pl.multiple_of(ck * half, half), half)
    theirs = pl.ds(pl.multiple_of(other_c * half, half), half)

    barrier = pltpu.get_barrier_semaphore()
    partners = [{C: other_c}, {Y: other_y}, {Y: other_y, C: other_c}]
    partners += [{X: turn(X, by)} for by in range(1, nx)]
    partners += [{Z: turn(Z, 1)}, {Z: turn(Z, -1)}]
    partners += [{ISLAND: turn(ISLAND, by)} for by in range(1, ni)]
    for partner in partners:
        pl.semaphore_signal(barrier, inc=1, device_id=partner, device_id_type=MESH_ID)
    a_out[...] = a_ref[...].astype(F32)
    g_out[...] = g_ref[:, theirs].astype(F32)
    p_out[...] = p_ref[...].astype(F32)
    pl.semaphore_wait(barrier, len(partners))

    got_g = lanes.send(g_out, g_in, **{C: other_c})
    got_a = lanes.send(a_out, a_in, **{C: other_c})
    got_p = [lanes.send(p_out, p_in.at[quad], **peer) for peer in partners[:3]]
    got_w = [
        lanes.send(w_ref, w_all.at[island], **{ISLAND: turn(ISLAND, by)})
        for by in range(1, ni)
    ]

    def product(a, g, add):
        wide = 11 * LANES
        count = wide // part_z.shape[2]
        for at in range(a.shape[1] // wide):
            lhs = a[:, at * wide : (at + 1) * wide].astype(jnp.bfloat16)
            out = lax.dot_general(
                lhs, g, (((0,), (0,)), ((), ())), preferred_element_type=F32
            )
            out = out.reshape(count, part_z.shape[2], half)
            block = at * count
            done = 0
            while done < count:
                x, z = divmod(block + done, nz)
                take = min(nz - z, count - done)
                for ref, cols in ((part_z, slice(0, LANES)), (part_x, slice(LANES, half))):
                    piece = out[done : done + take, :, cols]
                    if add:
                        piece = ref[x, z : z + take] + piece
                    ref[x, z : z + take] = piece
                done += take

    product(a_ref, g_ref[:, mine], False)
    p_in[quad] = p_out[...]
    got_g.wait_recv()
    got_a.wait_recv()
    product(a_in, g_in[...].astype(jnp.bfloat16), True)

    up_z, up_x = nz // 2, nx // 2
    first_z, first_x = [], []
    for sub in range(2):
        lead_z, lead_x = pl.ds(sub * (nx // 2), nx // 2), pl.ds(sub * (nz // 2), nz // 2)
        at_z = lambda d, lead=lead_z: part_z.at[lead, d]
        at_x = lambda d, lead=lead_x: part_x.at[d, lead]
        for way, z_slots, x_slots in ((1, z_up, x_up), (-1, z_down, x_down)):
            less = int((way == 1) == (sub == 1))
            first_z.append(chain(lanes, Z, up_z - less, way, at_z, z_slots.at[sub]))
            first_x.append(chain(lanes, X, up_x - less, way, at_x, x_slots.at[sub]))
    second_z = [
        chain(lanes, Z, up_z, 1, lambda d: part_x.at[xk, d], xz_up),
        chain(lanes, Z, up_z - 1, -1, lambda d: part_x.at[xk, d], xz_down),
    ]
    second_x = [
        chain(lanes, X, up_x, 1, lambda d: part_z.at[d, zk], zx_up),
        chain(lanes, X, up_x - 1, -1, lambda d: part_z.at[d, zk], zx_down),
    ]
    advance(first_z)
    advance(first_x)
    advance(first_z)
    advance(first_z)
    advance(first_x)
    advance(first_z)
    advance(first_z)
    advance(first_x)
    advance(second_z)
    advance(first_z)
    advance(second_z)
    advance(first_z)
    advance(second_x)
    advance(second_z)
    advance(second_x)
    advance(second_z)
    advance(second_x)
    got_yz = lanes.send(part_z.at[xk, zk], y_z, **{Y: other_y})
    for _ in range(3):
        advance(second_z)
    got_yx = lanes.send(part_x.at[xk, zk], y_x, **{Y: other_y})

    for j, copy in enumerate(got_p):
        copy.wait_recv()
    for j in range(4):
        p_all[j * rows : (j + 1) * rows, :] = p_in[j]

    got_yz.wait_recv()
    got_yx.wait_recv()
    grad[:, mine] = jnp.concatenate(
        [part_z[xk, zk] + y_z[...], part_x[xk, zk] + y_x[...]], axis=1
    )
    got_grad = lanes.send(grad.at[:, mine], grad.at[:, mine], **{C: other_c})

    proj_part[...] = lax.dot_general(
        p_all[...],
        grad[:, mine],
        (((0,), (0,)), ((), ())),
        precision=lax.Precision.HIGHEST,
        preferred_element_type=F32,
    ).reshape(proj_part.shape)
    got_x = [
        lanes.send(proj_part.at[turn(X, by)], proj_x.at[by - 1], **{X: turn(X, by)})
        for by in range(1, nx)
    ]

    got_grad.wait_recv()
    for j in range(4):
        @pl.when(quad == j)
        def _(j=j):
            grad_own[...] = grad[j * rows : (j + 1) * rows, :]
    got_gi = [
        lanes.send(grad_own, grad_all.at[island], **{ISLAND: turn(ISLAND, by)})
        for by in range(1, ni)
    ]

    own = proj_part[xk]
    for copy, by in zip(got_x, range(1, nx)):
        copy.wait_recv()
        own = own + proj_x[by - 1]
    proj_z[zk] = own

    ups, downs = [], []
    for step in range(up_z):
        for way, held, last in ((1, ups, up_z), (-1, downs, up_z - 1)):
            if step >= last:
                continue
            if held:
                held[-1].wait_recv()
            source = proj_z.at[turn(Z, -way * step)]
            held.append(lanes.send(source, source, **{Z: turn(Z, way)}))
    ups[-1].wait_recv()
    downs[-1].wait_recv()
    block = proj_z[0]
    for z in range(1, nz):
        block = block + proj_z[z]
    depth = block.shape[0]
    here = pl.ds(pl.multiple_of(xk * depth, depth), depth)
    new_first = first_decay * first_ref[here, mine] + (1.0 - first_decay) * block
    new_second = second_decay * second_ref[here, mine] + (1.0 - second_decay) * block * block
    adapted = new_first / first_fix / (jnp.sqrt(new_second / second_fix) + epsilon)
    stats[xk, 0:1] = jnp.sum(adapted * adapted, axis=0, keepdims=True)
    stats[xk, 1:2] = jnp.sum(block * block, axis=0, keepdims=True)
    got_stats = [
        lanes.send(stats.at[xk], stats.at[xk], **{X: turn(X, by)}) for by in range(1, nx)
    ]
    proj_all[xk, :, mine] = block
    got_proj = [
        lanes.send(
            proj_all.at[xk, :, mine], proj_all.at[xk, :, mine], **{X: turn(X, by)}
        )
        for by in range(1, nx)
    ]
    for copy in got_stats:
        copy.wait_recv()
    sums = stats[0]
    for x in range(1, nx):
        sums = sums + stats[x]
    sums = sums / RANK
    scales[ck] = jnp.sqrt(sums[0:1]) / jnp.sqrt(sums[1:2] + 1e-06)
    got_scale = lanes.send(scales.at[ck], scales.at[ck], **{C: other_c})
    got_scale.wait_recv()
    for core in range(2):
        scale_all[island, :, core * half : (core + 1) * half] = scales[core]
    got_si = [
        lanes.send(
            scale_all.at[island], scale_all.at[island], **{ISLAND: turn(ISLAND, by)}
        )
        for by in range(1, ni)
    ]

    for copy in got_proj:
        copy.wait_recv()
    got_half = lanes.send(
        proj_all.at[:, :, mine], proj_all.at[:, :, mine], **{C: other_c}
    )
    w_all[island] = w_ref[...]
    grad_all[island] = grad_own[...]
    for copy in got_w + got_gi:
        copy.wait_recv()
    got_half.wait_recv()
    proj_ref[...] = proj_all[...].reshape(proj_ref.shape)
    for copy in got_si:
        copy.wait_recv()
    total = None
    for i in range(ni):
        stepped = w_all[i] - inner_rate * grad_all[i] * scale_all[i]
        total = stepped if total is None else total + stepped
    total_ref[...] = total
    for copy in lanes.started:
        copy.wait_send()


def exchange(a, g, p, first, second, w):
    tokens, features = a.shape
    cols = g.shape[1]
    half = cols // 2
    rows = p.shape[0]
    nx, nz, ni = lax.axis_size(X), lax.axis_size(Z), lax.axis_size(ISLAND)
    quad = 4 * rows
    ups, downs = nz // 2, nz // 2 - 1
    vmem = lambda *shape: pltpu.VMEM(shape, F32)
    depth = RANK // nx
    scratch = [
        vmem(tokens, features), vmem(tokens, features),
        vmem(tokens, half), vmem(tokens, half),
        vmem(rows, RANK), vmem(4, rows, RANK), vmem(quad, RANK),
        vmem(nx, nz, quad, LANES), vmem(nx, nz, quad, LANES),
        vmem(2, ups, nx // 2, quad, LANES), vmem(2, ups, nx // 2, quad, LANES),
        vmem(2, nx // 2, nz // 2, quad, LANES), vmem(2, nx // 2, nz // 2, quad, LANES),
        vmem(nx // 2, quad, LANES), vmem(nx // 2, quad, LANES),
        vmem(ups, quad, LANES), vmem(ups, quad, LANES),
        vmem(quad, LANES), vmem(quad, LANES),
        vmem(quad, cols), vmem(rows, cols), vmem(ni, rows, cols), vmem(ni, rows, cols),
        vmem(nx, depth, half), vmem(nx - 1, depth, half), vmem(nz, depth, half),
        vmem(nx, depth, cols), vmem(nx, 2, half), vmem(2, 1, half), vmem(ni, 1, cols),
        pltpu.SemaphoreType.DMA((96,)),
        pltpu.SemaphoreType.DMA((96,)),
    ]
    return pl.pallas_call(
        comm_kernel,
        name="exchange",
        out_shape=(
            jax.ShapeDtypeStruct((RANK, cols), F32),
            jax.ShapeDtypeStruct((rows, cols), F32),
        ),
        in_specs=[pl.BlockSpec(memory_space=pltpu.VMEM)] * 6,
        out_specs=(pl.BlockSpec(memory_space=pltpu.VMEM),) * 2,
        scratch_shapes=scratch,
        compiler_params=pltpu.CompilerParams(
            collective_id=0, has_side_effects=True, vmem_limit_bytes=48 << 20
        ),
    )(a, g, p, first, second, w)


def body(
    activations,
    out_grads,
    projection,
    first_moment,
    second_moment,
    inner_weights,
    global_weights,
    outer_momentum,
):
    projected, stepped_sum = exchange(
        activations[0],
        out_grads[0],
        projection,
        first_moment[0, 0],
        second_moment[0, 0],
        inner_weights[0],
    )
    new_first = first_decay * first_moment[0, 0] + (1.0 - first_decay) * projected
    new_second = (
        second_decay * second_moment[0, 0] + (1.0 - second_decay) * projected * projected
    )
    island_count = lax.axis_size(ISLAND)
    pseudo_grad = global_weights - stepped_sum / island_count
    new_momentum = outer_beta * outer_momentum + pseudo_grad
    weights_next = (
        global_weights - outer_rate * (pseudo_grad + outer_beta * new_momentum)
    ).astype(jnp.bfloat16)
    block_cols = global_weights.shape[1] // island_count
    weights_block = lax.dynamic_slice_in_dim(
        weights_next, lax.axis_index(ISLAND) * block_cols, block_cols, 1
    )
    return (weights_block, new_momentum, new_first[None, None], new_second[None, None])


def solution(mesh):
    torus = Mesh(
        mesh.devices.reshape(4, 12, 2, 2, mesh.shape["island"]),
        (*FSDP, ISLAND),
    )
    placed = (
        P(ISLAND, FSDP, None),
        P(ISLAND, FSDP, None),
        P(FSDP, None),
        P(ISLAND, None, None, None),
        P(ISLAND, None, None, None),
        P(ISLAND, FSDP, None),
        P(FSDP, None),
        P(FSDP, None),
    )
    return jax.shard_map(
        body,
        mesh=torus,
        in_specs=placed,
        out_specs=(
            P(FSDP, ISLAND),
            P(FSDP, None),
            P(ISLAND, None, None, None),
            P(ISLAND, None, None, None),
        ),
        check_vma=False,
    )
```

```python
import functools

import jax
import jax.numpy as jnp
from jax import lax
from jax.experimental import pallas as pl
from jax.experimental.pallas import tpu as pltpu
from jax.sharding import Mesh
from jax.sharding import PartitionSpec as P

RANK = 256
X, Z, Y, C = "fsdp_0", "fsdp_1", "fsdp_2", "fsdp_3"
ISLAND = "island"
FSDP = (X, Z, Y, C)
LANES = 128
MESH_ID = pl.DeviceIdType.MESH
F32 = jnp.float32

first_decay = 0.9
second_decay = 0.999
first_fix = 1.0 - 0.9**10
second_fix = 1.0 - 0.999**10
epsilon = 1e-08
inner_rate = 1.0
outer_rate = 0.7
outer_beta = 0.9


class Lanes:
    def __init__(self, send_sems, recv_sems):
        self.send_sems, self.recv_sems = send_sems, recv_sems
        self.used = 0
        self.started = []

    def send(self, src, dst, **peer):
        copy = pltpu.make_async_remote_copy(
            src_ref=src,
            dst_ref=dst,
            send_sem=self.send_sems.at[self.used],
            recv_sem=self.recv_sems.at[self.used],
            device_id=peer,
            device_id_type=MESH_ID,
        )
        self.used += 1
        copy.start()
        self.started.append(copy)
        return copy


def turn(axis, by):
    size = lax.axis_size(axis)
    return lax.rem(lax.axis_index(axis) + by + size, size)


def chain(lanes, axis, steps, way, block, slots):
    copy = None
    for step in range(steps):
        at = block(turn(axis, way * (steps - step)))
        if copy is not None:
            copy.wait_recv()
            at[...] = at[...] + slots[step - 1]
        copy = lanes.send(at, slots.at[step], **{axis: turn(axis, way)})
        yield
    copy.wait_recv()
    at = block(lax.axis_index(axis))
    at[...] = at[...] + slots[steps - 1]


def advance(chains):
    for one in chains:
        next(one, None)


def comm_kernel(
    a_hbm, g_hbm, p_hbm, first_hbm, second_hbm, w_hbm,
    proj_ref, total_ref,
    a_ref, g_ref, p_ref, first_ref, second_ref,
    a_out, a_in, g_out, g_in, p_out, p_in, p_all,
    part_z, part_x,
    z_up, z_down, xa_up, xa_down, xb_up, xb_down,
    zx_up, zx_down, sa_up, sa_down, sb_up, sb_down,
    y_z, y_x, grad, grad_own, w_all, grad_all,
    proj_part, proj_x, proj_z, proj_all, stats, scale_all,
    send_sems, recv_sems, load_sems,
):
    xk, zk, yk, ck = (lax.axis_index(name) for name in FSDP)
    island = lax.axis_index(ISLAND)
    nx, nz = lax.axis_size(X), lax.axis_size(Z)
    ni = lax.axis_size(ISLAND)
    lanes = Lanes(send_sems, recv_sems)
    other_c, other_y = 1 - ck, 1 - yk
    quad = yk * 2 + ck
    half = g_ref.shape[1] // 2
    depth = first_ref.shape[0]
    rows = p_ref.shape[0]
    height = part_z.shape[2]
    mine = pl.ds(pl.multiple_of(ck * half, half), half)
    theirs = pl.ds(pl.multiple_of(other_c * half, half), half)
    here = pl.ds(pl.multiple_of((xk * 2 + yk) * depth, depth), depth)

    def near(by_x, by_y, by_c=0):
        peer = {}
        if by_x:
            peer[X] = turn(X, by_x)
        if by_y:
            peer[Y] = other_y
        if by_c:
            peer[C] = other_c
        return peer

    moves = [
        (g_hbm, g_ref), (a_hbm, a_ref), (p_hbm, p_ref),
        (w_hbm, w_all.at[island]),
        (first_hbm.at[here, mine], first_ref), (second_hbm.at[here, mine], second_ref),
    ]
    loads = [
        pltpu.make_async_copy(src, dst, load_sems.at[at])
        for at, (src, dst) in enumerate(moves)
    ]
    for load in loads:
        load.start()

    barrier = pltpu.get_barrier_semaphore()
    around = [
        near(i % nx, i // nx % 2, i // (2 * nx)) for i in range(1, 4 * nx)
    ]
    partners = around + [{Z: turn(Z, 1)}, {Z: turn(Z, -1)}]
    partners += [{ISLAND: turn(ISLAND, by)} for by in range(1, ni)]
    for partner in partners:
        pl.semaphore_signal(barrier, inc=1, device_id=partner, device_id_type=MESH_ID)
    loads[0].wait()
    g_out[...] = g_ref[:, theirs].astype(F32)
    loads[1].wait()
    a_out[...] = a_ref[...].astype(F32)
    loads[2].wait()
    p_out[...] = p_ref[...].astype(F32)
    pl.semaphore_wait(barrier, len(partners))

    wide = 11 * LANES
    spans = [slice(at, at + wide) for at in range(0, a_ref.shape[1], wide)]
    got_g = lanes.send(g_out, g_in, **{C: other_c})
    got_a = [lanes.send(a_out.at[:, at], a_in.at[:, at], **{C: other_c}) for at in spans]
    got_p = [
        lanes.send(p_out, p_in.at[quad], **near(0, y, c)) for y, c in ((0, 1), (1, 0), (1, 1))
    ]
    got_w = [
        lanes.send(w_hbm, w_all.at[island], **{ISLAND: turn(ISLAND, by)})
        for by in range(1, ni)
    ]

    def product(a, g, span, add):
        count = wide // height
        lhs = a[:, span].astype(jnp.bfloat16)
        out = lax.dot_general(lhs, g, (((0,), (0,)), ((), ())), preferred_element_type=F32)
        out = out.reshape(count, height, half)
        block = span.start // height
        done = 0
        while done < count:
            x, z = divmod(block + done, nz)
            take = min(nz - z, count - done)
            for ref, cols in ((part_z, slice(0, LANES)), (part_x, slice(LANES, half))):
                piece = out[done : done + take, :, cols]
                if add:
                    piece = ref[x, z : z + take] + piece
                ref[x, z : z + take] = piece
            done += take

    for span in spans:
        product(a_ref, g_ref[:, mine], span, False)
    p_in[quad] = p_out[...]
    got_g.wait_recv()
    for copy, span in zip(got_a, spans):
        copy.wait_recv()
        product(a_in, g_in[...].astype(jnp.bfloat16), span, True)

    up_z, up_x = nz // 2, nx // 2
    cut = xa_up.shape[3]
    both = ((1, 0), (-1, 1))
    chain_z, chain_a, chain_b = [], [], []
    for sub in range(nx):
        block = lambda d, sub=sub: part_z.at[sub, d]
        for way, slots in ((1, z_up), (-1, z_down)):
            less = int((way == 1) == (sub % 2 == 1))
            chain_z.append(chain(lanes, Z, up_z - less, way, block, slots.at[sub]))
    for chains, up, down, span in (
        (chain_a, xa_up, xa_down, slice(0, cut)),
        (chain_b, xb_up, xb_down, slice(cut, height)),
    ):
        for sub in range(2):
            lead = slice(sub * (nz // 2), (sub + 1) * (nz // 2))
            block = lambda d, lead=lead, span=span: part_x.at[d, lead, span]
            for way, slots in ((1, up), (-1, down)):
                less = int((way == 1) == (sub == 1))
                chains.append(chain(lanes, X, up_x - less, way, block, slots.at[sub]))
    block_a = lambda d: part_x.at[xk, d, slice(0, cut)]
    block_b = lambda d: part_x.at[xk, d, slice(cut, height)]
    block_z = lambda d: part_z.at[d, zk]
    last_a = [
        chain(lanes, Z, up_z - less, way, block_a, slots)
        for (way, less), slots in zip(both, (sa_up, sa_down))
    ]
    last_b = [
        chain(lanes, Z, up_z - 1 + less, way, block_b, slots)
        for (way, less), slots in zip(both, (sb_up, sb_down))
    ]
    last_z = [
        chain(lanes, X, up_x - less, way, block_z, slots)
        for (way, less), slots in zip(both, (zx_up, zx_down))
    ]
    order = [
        chain_z, chain_a, chain_z, chain_a, chain_b, chain_z,
        chain_a, last_a, chain_b, chain_z, last_a, chain_z, last_a,
        chain_b, last_b, chain_z, last_a, last_b, chain_z,
        last_z, last_a, last_b, last_z, last_a, last_b, last_z,
    ]
    for chains in order:
        advance(chains)
    got_yz = lanes.send(part_z.at[xk, zk], y_z, **{Y: other_y})
    for copy in got_p:
        copy.wait_recv()
    for j in range(4):
        p_all[j * rows : (j + 1) * rows, :] = p_in[j]
    advance(last_a)
    for _ in range(3):
        advance(last_b)

    proj_part[...] = lax.dot_general(
        p_all[...],
        jnp.concatenate([part_z[xk, zk], part_x[xk, zk]], axis=1),
        (((0,), (0,)), ((), ())),
        precision=lax.Precision.HIGHEST,
        preferred_element_type=F32,
    ).reshape(proj_part.shape)
    got_x = []
    for i in range(1, 2 * nx):
        by_x, by_y = i % nx, i // nx
        to_x = turn(X, by_x)
        to_y = other_y if by_y else yk
        got_x.append(
            lanes.send(proj_part.at[to_x, to_y], proj_x.at[i - 1], **near(by_x, by_y))
        )

    got_yx = lanes.send(part_x.at[xk, zk], y_x, **{Y: other_y})
    own = proj_part[xk, yk]
    for i, copy in enumerate(got_x):
        copy.wait_recv()
        own = own + proj_x[i]
    proj_z[zk] = own

    ups, downs = [], []
    for step in range(up_z):
        for way, held, last in ((1, ups, up_z), (-1, downs, up_z - 1)):
            if step >= last:
                continue
            if held:
                held[-1].wait_recv()
            source = proj_z.at[turn(Z, -way * step)]
            held.append(lanes.send(source, source, **{Z: turn(Z, way)}))
        if step == 0:
            got_yz.wait_recv()
            got_yx.wait_recv()
            grad[:, mine] = jnp.concatenate(
                [part_z[xk, zk] + y_z[...], part_x[xk, zk] + y_x[...]], axis=1
            )
            got_grad = lanes.send(grad.at[:, mine], grad.at[:, mine], **{C: other_c})
        if step == 1:
            got_grad.wait_recv()
            for j in range(4):
                @pl.when(quad == j)
                def _(j=j):
                    grad_own[...] = grad[j * rows : (j + 1) * rows, :]
            got_gi = [
                lanes.send(grad_own, grad_all.at[island], **{ISLAND: turn(ISLAND, by)})
                for by in range(1, ni)
            ]
    grad_all[island] = grad_own[...]
    for load in loads[3:]:
        load.wait()
    ups[-1].wait_recv()
    downs[-1].wait_recv()
    block = proj_z[0]
    for z in range(1, nz):
        block = block + proj_z[z]
    new_first = first_decay * first_ref[...] + (1.0 - first_decay) * block
    new_second = second_decay * second_ref[...] + (1.0 - second_decay) * block * block
    adapted = new_first / first_fix / (jnp.sqrt(new_second / second_fix) + epsilon)
    place = (ck * nx + xk) * 2 + yk
    stats[place, 0:1] = jnp.sum(adapted * adapted, axis=0, keepdims=True)
    stats[place, 1:2] = jnp.sum(block * block, axis=0, keepdims=True)
    got_stats = [lanes.send(stats.at[place], stats.at[place], **peer) for peer in around]
    proj_all[xk, yk, :, mine] = block
    got_proj = []
    for by in range(1, nx):
        spot = proj_all.at[xk, yk, :, mine]
        got_proj.append(lanes.send(spot, spot, **{X: turn(X, by)}))
    for copy in got_stats:
        copy.wait_recv()
    for core in range(2):
        sums = stats[2 * nx * core]
        for i in range(1, 2 * nx):
            sums = sums + stats[2 * nx * core + i]
        sums = sums / RANK
        scale_all[island, :, core * half : (core + 1) * half] = jnp.sqrt(
            sums[0:1]
        ) / jnp.sqrt(sums[1:2] + 1e-06)
    got_si = [
        lanes.send(
            scale_all.at[island], scale_all.at[island], **{ISLAND: turn(ISLAND, by)}
        )
        for by in range(1, ni)
    ]

    for copy in got_proj:
        copy.wait_recv()
    spot = proj_all.at[:, yk, :, mine]
    got_far = lanes.send(spot, spot, **{Y: other_y})
    got_close = lanes.send(spot, spot, **{C: other_c})
    for copy in got_w + got_gi:
        copy.wait_recv()
    weights = w_all[0]
    for i in range(1, ni):
        weights = weights + w_all[i]
    weights = weights.reshape(rows, grad_own.shape[1])
    got_far.wait_recv()
    spot = proj_all.at[:, other_y, :, mine]
    got_last = lanes.send(spot, spot, **{C: other_c})
    for copy in got_si:
        copy.wait_recv()
    moved = None
    for i in range(ni):
        step = inner_rate * grad_all[i] * scale_all[i]
        moved = step if moved is None else moved + step
    total_ref[...] = weights - moved
    got_close.wait_recv()
    got_last.wait_recv()
    proj_ref[...] = proj_all[...].reshape(proj_ref.shape)
    for copy in lanes.started:
        copy.wait_send()


def exchange(a, g, p, first, second, w):
    tokens, features = a.shape
    cols = g.shape[1]
    half = cols // 2
    rows = p.shape[0]
    nx, nz, ni = lax.axis_size(X), lax.axis_size(Z), lax.axis_size(ISLAND)
    quad = 4 * rows
    cut = quad // 16 * 8 + 8
    ups, upx = nz // 2, nx // 2
    vmem = lambda *shape: pltpu.VMEM(shape, F32)
    depth = RANK // nx // 2
    scratch = [
        pltpu.VMEM(a.shape, a.dtype), pltpu.VMEM(g.shape, g.dtype), pltpu.VMEM(p.shape, p.dtype),
        vmem(depth, half), vmem(depth, half),
        vmem(tokens, features), vmem(tokens, features),
        vmem(tokens, half), vmem(tokens, half),
        vmem(rows, RANK), vmem(4, rows, RANK), vmem(quad, RANK),
        vmem(nx, nz, quad, LANES), vmem(nx, nz, quad, LANES),
        vmem(nx, ups, quad, LANES), vmem(nx, ups, quad, LANES),
        vmem(2, upx, nz // 2, cut, LANES), vmem(2, upx, nz // 2, cut, LANES),
        vmem(2, upx, nz // 2, quad - cut, LANES), vmem(2, upx, nz // 2, quad - cut, LANES),
        vmem(upx, quad, LANES), vmem(upx, quad, LANES),
        vmem(ups, cut, LANES), vmem(ups, cut, LANES),
        vmem(ups, quad - cut, LANES), vmem(ups, quad - cut, LANES),
        vmem(quad, LANES), vmem(quad, LANES),
        vmem(quad, cols), vmem(rows, cols),
        vmem(ni, *w.shape), vmem(ni, rows, cols),
        vmem(nx, 2, depth, half), vmem(2 * nx - 1, depth, half), vmem(nz, depth, half),
        vmem(nx, 2, depth, cols), vmem(4 * nx, 2, half), vmem(ni, 1, cols),
        pltpu.SemaphoreType.DMA((150,)),
        pltpu.SemaphoreType.DMA((150,)),
        pltpu.SemaphoreType.DMA((6,)),
    ]
    return pl.pallas_call(
        comm_kernel,
        name="exchange",
        out_shape=(
            jax.ShapeDtypeStruct((RANK, cols), F32),
            jax.ShapeDtypeStruct((rows, cols), F32),
        ),
        in_specs=[pl.BlockSpec(memory_space=pltpu.HBM)] * 6,
        out_specs=(pl.BlockSpec(memory_space=pltpu.VMEM),) * 2,
        scratch_shapes=scratch,
        compiler_params=pltpu.CompilerParams(
            collective_id=0, has_side_effects=True, vmem_limit_bytes=67043328
        ),
    )(a, g, p, first, second, w)


def body(
    activations,
    out_grads,
    projection,
    first_moment,
    second_moment,
    inner_weights,
    global_weights,
    outer_momentum,
):
    projected, stepped_sum = exchange(
        activations[0],
        out_grads[0],
        projection,
        first_moment[0, 0],
        second_moment[0, 0],
        inner_weights.reshape(-1, 1, inner_weights.shape[2]),
    )
    new_first = first_decay * first_moment[0, 0] + (1.0 - first_decay) * projected
    new_second = (
        second_decay * second_moment[0, 0] + (1.0 - second_decay) * projected * projected
    )
    island_count = lax.axis_size(ISLAND)
    pseudo_grad = global_weights - stepped_sum / island_count
    new_momentum = outer_beta * outer_momentum + pseudo_grad
    weights_next = (
        global_weights - outer_rate * (pseudo_grad + outer_beta * new_momentum)
    ).astype(jnp.bfloat16)
    block_cols = global_weights.shape[1] // island_count
    weights_block = lax.dynamic_slice_in_dim(
        weights_next, lax.axis_index(ISLAND) * block_cols, block_cols, 1
    )
    return (weights_block, new_momentum, new_first[None, None], new_second[None, None])


def solution(mesh):
    torus = Mesh(
        mesh.devices.reshape(4, 12, 2, 2, mesh.shape["island"]),
        (*FSDP, ISLAND),
    )
    placed = (
        P(ISLAND, FSDP, None),
        P(ISLAND, FSDP, None),
        P(FSDP, None),
        P(ISLAND, None, None, None),
        P(ISLAND, None, None, None),
        P(ISLAND, FSDP, None),
        P(FSDP, None),
        P(FSDP, None),
    )
    return jax.shard_map(
        body,
        mesh=torus,
        in_specs=placed,
        out_specs=(
            P(FSDP, ISLAND),
            P(FSDP, None),
            P(ISLAND, None, None, None),
            P(ISLAND, None, None, None),
        ),
        check_vma=False,
    )
```

```python
import functools

import jax
import jax.numpy as jnp
from jax import lax
from jax.experimental import pallas as pl
from jax.experimental.pallas import tpu as pltpu
from jax.sharding import Mesh
from jax.sharding import PartitionSpec as P

RANK = 256
X, Z, Y, C = "fsdp_0", "fsdp_1", "fsdp_2", "fsdp_3"
ISLAND = "island"
FSDP = (X, Z, Y, C)
LANES = 128
RING_ORDER = (
    "iljkmpnoadehbcfgadehilbcgfajkdehcbmpgfadonehcbgi",
    "lqrfadehmptscbrgqfadehstcbrgqfadehuvstqrstuvqrst",
    "qrustqt",
)
MESH_ID = pl.DeviceIdType.MESH
F32 = jnp.float32

first_decay = 0.9
second_decay = 0.999
first_fix = 1.0 - 0.9**10
second_fix = 1.0 - 0.999**10
epsilon = 1e-08
inner_rate = 1.0
outer_rate = 0.7
outer_beta = 0.9


class Lanes:
    def __init__(self, send_sems, recv_sems):
        self.send_sems, self.recv_sems = send_sems, recv_sems
        self.used = 0
        self.started = []

    def send(self, src, dst, **peer):
        copy = pltpu.make_async_remote_copy(
            src_ref=src,
            dst_ref=dst,
            send_sem=self.send_sems.at[self.used],
            recv_sem=self.recv_sems.at[self.used],
            device_id=peer,
            device_id_type=MESH_ID,
        )
        self.used += 1
        copy.start()
        self.started.append(copy)
        return copy


def turn(axis, by):
    size = lax.axis_size(axis)
    return lax.rem(lax.axis_index(axis) + by + size, size)


def chain(lanes, axis, steps, way, block, slots):
    copy = None
    for step in range(steps):
        at = block(turn(axis, way * (steps - step)))
        if copy is not None:
            copy.wait_recv()
            at[...] = at[...] + slots[step - 1]
        copy = lanes.send(at, slots.at[step], **{axis: turn(axis, way)})
        yield
    copy.wait_recv()
    at = block(lax.axis_index(axis))
    at[...] = at[...] + slots[steps - 1]


def advance(chains):
    for one in chains:
        next(one, None)


def comm_kernel(
    a_hbm, g_hbm, p_hbm, first_hbm, second_hbm, w_hbm,
    proj_ref, total_ref,
    a_ref, g_ref, p_ref, first_ref, second_ref,
    a_out, a_in, g_out, g_in, p_out, p_in, p_all,
    part_z, part_x,
    z_up, z_down, xa_up, xa_down, xb_up, xb_down,
    zx_up, zx_down, sa_up, sa_down, sb_up, sb_down,
    y_z, y_x, grad, grad_own, w_all, grad_all,
    proj_part, proj_x, proj_z, proj_all, stats, scale_all,
    send_sems, recv_sems, load_sems,
):
    xk, zk, yk, ck = (lax.axis_index(name) for name in FSDP)
    island = lax.axis_index(ISLAND)
    nx, nz = lax.axis_size(X), lax.axis_size(Z)
    ni = lax.axis_size(ISLAND)
    lanes = Lanes(send_sems, recv_sems)
    other_c, other_y = 1 - ck, 1 - yk
    quad = yk * 2 + ck
    half = g_ref.shape[1] // 2
    depth = first_ref.shape[0]
    rows = p_ref.shape[0]
    height = part_z.shape[2]
    mine = pl.ds(pl.multiple_of(ck * half, half), half)
    theirs = pl.ds(pl.multiple_of(other_c * half, half), half)
    here = pl.ds(pl.multiple_of((xk * 2 + yk) * depth, depth), depth)

    def near(by_x, by_y, by_c=0):
        peer = {}
        if by_x:
            peer[X] = turn(X, by_x)
        if by_y:
            peer[Y] = other_y
        if by_c:
            peer[C] = other_c
        return peer

    moves = [
        (g_hbm, g_ref), (a_hbm, a_ref), (p_hbm, p_ref),
        (w_hbm, w_all.at[island]),
        (first_hbm.at[here, mine], first_ref), (second_hbm.at[here, mine], second_ref),
    ]
    loads = [
        pltpu.make_async_copy(src, dst, load_sems.at[at])
        for at, (src, dst) in enumerate(moves)
    ]
    for load in loads:
        load.start()

    barrier = pltpu.get_barrier_semaphore()
    around = [
        near(i % nx, i // nx % 2, i // (2 * nx)) for i in range(1, 4 * nx)
    ]
    partners = around + [{Z: turn(Z, 1)}, {Z: turn(Z, -1)}]
    partners += [{ISLAND: turn(ISLAND, by)} for by in range(1, ni)]
    for partner in partners:
        pl.semaphore_signal(barrier, inc=1, device_id=partner, device_id_type=MESH_ID)
    loads[0].wait()
    g_out[...] = g_ref[:, theirs].astype(F32)
    loads[1].wait()
    a_out[...] = a_ref[...].astype(F32)
    loads[2].wait()
    p_out[...] = p_ref[...].astype(F32)
    pl.semaphore_wait(barrier, len(partners))

    wide = 11 * LANES
    spans = [slice(at, at + wide) for at in range(0, a_ref.shape[1], wide)]
    got_g = lanes.send(g_out, g_in, **{C: other_c})
    got_a = [lanes.send(a_out.at[:, at], a_in.at[:, at], **{C: other_c}) for at in spans]
    got_p = [
        lanes.send(p_out, p_in.at[quad], **near(0, y, c)) for y, c in ((0, 1), (1, 0), (1, 1))
    ]
    got_w = [
        lanes.send(w_hbm, w_all.at[island], **{ISLAND: turn(ISLAND, by)})
        for by in range(1, ni)
    ]

    def product(a, g, span, add):
        count = wide // height
        lhs = a[:, span].astype(jnp.bfloat16)
        out = lax.dot_general(lhs, g, (((0,), (0,)), ((), ())), preferred_element_type=F32)
        out = out.reshape(count, height, half)
        block = span.start // height
        done = 0
        while done < count:
            x, z = divmod(block + done, nz)
            take = min(nz - z, count - done)
            for ref, cols in ((part_z, slice(0, LANES)), (part_x, slice(LANES, half))):
                piece = out[done : done + take, :, cols]
                if add:
                    piece = ref[x, z : z + take] + piece
                ref[x, z : z + take] = piece
            done += take

    for span in spans:
        product(a_ref, g_ref[:, mine], span, False)
    p_in[quad] = p_out[...]
    got_g.wait_recv()
    for copy, span in zip(got_a, spans):
        copy.wait_recv()
        product(a_in, g_in[...].astype(jnp.bfloat16), span, True)

    up_z, up_x = nz // 2, nx // 2
    cut = xa_up.shape[3]
    both = ((1, 0), (-1, 1))
    chain_z, chain_a, chain_b = [], [], []
    for sub in range(nx):
        block = lambda d, sub=sub: part_z.at[sub, d]
        for way, slots in ((1, z_up), (-1, z_down)):
            less = int((way == 1) == (sub % 2 == 1))
            chain_z.append(chain(lanes, Z, up_z - less, way, block, slots.at[sub]))
    for chains, up, down, span in (
        (chain_a, xa_up, xa_down, slice(0, cut)),
        (chain_b, xb_up, xb_down, slice(cut, height)),
    ):
        for sub in range(2):
            lead = slice(sub * (nz // 2), (sub + 1) * (nz // 2))
            block = lambda d, lead=lead, span=span: part_x.at[d, lead, span]
            for way, slots in ((1, up), (-1, down)):
                less = int((way == 1) == (sub == 1))
                chains.append(chain(lanes, X, up_x - less, way, block, slots.at[sub]))
    block_a = lambda d: part_x.at[xk, d, slice(0, cut)]
    block_b = lambda d: part_x.at[xk, d, slice(cut, height)]
    block_z = lambda d: part_z.at[d, zk]
    last_a = [
        chain(lanes, Z, up_z - less, way, block_a, slots)
        for (way, less), slots in zip(both, (sa_up, sa_down))
    ]
    last_b = [
        chain(lanes, Z, up_z - 1 + less, way, block_b, slots)
        for (way, less), slots in zip(both, (sb_up, sb_down))
    ]
    last_z = [
        chain(lanes, X, up_x - less, way, block_z, slots)
        for (way, less), slots in zip(both, (zx_up, zx_down))
    ]
    every = chain_z + chain_a + chain_b + last_a + last_b + last_z
    for letter in "".join(RING_ORDER):
        at = ord(letter) - ord("a")
        advance([every[at]])
    for chains in (chain_z, chain_a, chain_b, last_a, last_b, last_z):
        for _ in range(up_z + 1):
            advance(chains)
    got_yz = lanes.send(part_z.at[xk, zk], y_z, **{Y: other_y})
    got_yx = lanes.send(part_x.at[xk, zk], y_x, **{Y: other_y})
    for copy in got_p:
        copy.wait_recv()
    for j in range(4):
        p_all[j * rows : (j + 1) * rows, :] = p_in[j]

    proj_part[...] = lax.dot_general(
        p_all[...],
        jnp.concatenate([part_z[xk, zk], part_x[xk, zk]], axis=1),
        (((0,), (0,)), ((), ())),
        precision=lax.Precision.HIGHEST,
        preferred_element_type=F32,
    ).reshape(proj_part.shape)
    got_x = []
    for i in range(1, 2 * nx):
        by_x, by_y = i % nx, i // nx
        to_x = turn(X, by_x)
        to_y = other_y if by_y else yk
        got_x.append(
            lanes.send(proj_part.at[to_x, to_y], proj_x.at[i - 1], **near(by_x, by_y))
        )

    got_yz.wait_recv()
    got_yx.wait_recv()
    grad[:, mine] = jnp.concatenate(
        [part_z[xk, zk] + y_z[...], part_x[xk, zk] + y_x[...]], axis=1
    )
    got_grad = lanes.send(grad.at[:, mine], grad.at[:, mine], **{C: other_c})
    own = proj_part[xk, yk]
    for i, copy in enumerate(got_x):
        copy.wait_recv()
        own = own + proj_x[i]
    proj_z[zk] = own

    ups, downs = [], []
    for step in range(up_z):
        for way, held, last in ((1, ups, up_z), (-1, downs, up_z - 1)):
            if step >= last:
                continue
            if held:
                held[-1].wait_recv()
            source = proj_z.at[turn(Z, -way * step)]
            held.append(lanes.send(source, source, **{Z: turn(Z, way)}))
        if step == 2:
            got_grad.wait_recv()
            for j in range(4):
                @pl.when(quad == j)
                def _(j=j):
                    grad_own[...] = grad[j * rows : (j + 1) * rows, :]
            got_gi = [
                lanes.send(grad_own, grad_all.at[island], **{ISLAND: turn(ISLAND, by)})
                for by in range(1, ni)
            ]
    grad_all[island] = grad_own[...]
    for load in loads[3:]:
        load.wait()
    ups[-1].wait_recv()
    downs[-1].wait_recv()
    block = proj_z[0]
    for z in range(1, nz):
        block = block + proj_z[z]
    new_first = first_decay * first_ref[...] + (1.0 - first_decay) * block
    new_second = second_decay * second_ref[...] + (1.0 - second_decay) * block * block
    adapted = new_first / first_fix / (jnp.sqrt(new_second / second_fix) + epsilon)
    place = (ck * nx + xk) * 2 + yk
    stats[place, 0:1] = jnp.sum(adapted * adapted, axis=0, keepdims=True)
    stats[place, 1:2] = jnp.sum(block * block, axis=0, keepdims=True)
    got_stats = [lanes.send(stats.at[place], stats.at[place], **peer) for peer in around]
    proj_all[xk, yk, :, mine] = block
    got_proj = []
    for i in range(1, 2 * nx):
        spot = proj_all.at[xk, yk, :, mine]
        got_proj.append(lanes.send(spot, spot, **near(i % nx, i // nx)))
    for copy in got_stats:
        copy.wait_recv()
    for core in range(2):
        sums = stats[2 * nx * core]
        for i in range(1, 2 * nx):
            sums = sums + stats[2 * nx * core + i]
        sums = sums / RANK
        scale_all[island, :, core * half : (core + 1) * half] = jnp.sqrt(
            sums[0:1]
        ) / jnp.sqrt(sums[1:2] + 1e-06)
    got_si = [
        lanes.send(
            scale_all.at[island], scale_all.at[island], **{ISLAND: turn(ISLAND, by)}
        )
        for by in range(1, ni)
    ]

    for copy in got_proj:
        copy.wait_recv()
    spot = proj_all.at[:, :, :, mine]
    got_close = lanes.send(spot, spot, **{C: other_c})
    for copy in got_w + got_gi:
        copy.wait_recv()
    weights = w_all[0]
    for i in range(1, ni):
        weights = weights + w_all[i]
    weights = weights.reshape(rows, grad_own.shape[1])
    for copy in got_si:
        copy.wait_recv()
    moved = None
    for i in range(ni):
        step = inner_rate * grad_all[i] * scale_all[i]
        moved = step if moved is None else moved + step
    total_ref[...] = weights - moved
    got_close.wait_recv()
    proj_ref[...] = proj_all[...].reshape(proj_ref.shape)
    for copy in lanes.started:
        copy.wait_send()


def exchange(a, g, p, first, second, w):
    tokens, features = a.shape
    cols = g.shape[1]
    half = cols // 2
    rows = p.shape[0]
    nx, nz, ni = lax.axis_size(X), lax.axis_size(Z), lax.axis_size(ISLAND)
    quad = 4 * rows
    cut = quad // 16 * 8 + 8
    ups, upx = nz // 2, nx // 2
    vmem = lambda *shape: pltpu.VMEM(shape, F32)
    depth = RANK // nx // 2
    scratch = [
        pltpu.VMEM(a.shape, a.dtype), pltpu.VMEM(g.shape, g.dtype), pltpu.VMEM(p.shape, p.dtype),
        vmem(depth, half), vmem(depth, half),
        vmem(tokens, features), vmem(tokens, features),
        vmem(tokens, half), vmem(tokens, half),
        vmem(rows, RANK), vmem(4, rows, RANK), vmem(quad, RANK),
        vmem(nx, nz, quad, LANES), vmem(nx, nz, quad, LANES),
        vmem(nx, ups, quad, LANES), vmem(nx, ups, quad, LANES),
        vmem(2, upx, nz // 2, cut, LANES), vmem(2, upx, nz // 2, cut, LANES),
        vmem(2, upx, nz // 2, quad - cut, LANES), vmem(2, upx, nz // 2, quad - cut, LANES),
        vmem(upx, quad, LANES), vmem(upx, quad, LANES),
        vmem(ups, cut, LANES), vmem(ups, cut, LANES),
        vmem(ups, quad - cut, LANES), vmem(ups, quad - cut, LANES),
        vmem(quad, LANES), vmem(quad, LANES),
        vmem(quad, cols), vmem(rows, cols),
        vmem(ni, *w.shape), vmem(ni, rows, cols),
        vmem(nx, 2, depth, half), vmem(2 * nx - 1, depth, half), vmem(nz, depth, half),
        vmem(nx, 2, depth, cols), vmem(4 * nx, 2, half), vmem(ni, 1, cols),
        pltpu.SemaphoreType.DMA((150,)),
        pltpu.SemaphoreType.DMA((150,)),
        pltpu.SemaphoreType.DMA((6,)),
    ]
    return pl.pallas_call(
        comm_kernel,
        name="exchange",
        out_shape=(
            jax.ShapeDtypeStruct((RANK, cols), F32),
            jax.ShapeDtypeStruct((rows, cols), F32),
        ),
        in_specs=[pl.BlockSpec(memory_space=pltpu.HBM)] * 6,
        out_specs=(pl.BlockSpec(memory_space=pltpu.VMEM),) * 2,
        scratch_shapes=scratch,
        compiler_params=pltpu.CompilerParams(
            collective_id=0, has_side_effects=True, vmem_limit_bytes=40 << 20
        ),
    )(*(pltpu.with_memory_space_constraint(v, pltpu.HBM) for v in (a, g, p, first, second, w)))


def body(
    activations,
    out_grads,
    projection,
    first_moment,
    second_moment,
    inner_weights,
    global_weights,
    outer_momentum,
):
    projected, stepped_sum = exchange(
        activations[0],
        out_grads[0],
        projection,
        first_moment[0, 0],
        second_moment[0, 0],
        inner_weights.reshape(-1, 1, inner_weights.shape[2]),
    )
    new_first = first_decay * first_moment[0, 0] + (1.0 - first_decay) * projected
    new_second = (
        second_decay * second_moment[0, 0] + (1.0 - second_decay) * projected * projected
    )
    island_count = lax.axis_size(ISLAND)
    pseudo_grad = global_weights - stepped_sum / island_count
    new_momentum = outer_beta * outer_momentum + pseudo_grad
    weights_next = (
        global_weights - outer_rate * (pseudo_grad + outer_beta * new_momentum)
    ).astype(jnp.bfloat16)
    block_cols = global_weights.shape[1] // island_count
    weights_block = lax.dynamic_slice_in_dim(
        weights_next, lax.axis_index(ISLAND) * block_cols, block_cols, 1
    )
    return (weights_block, new_momentum, new_first[None, None], new_second[None, None])


def solution(mesh):
    torus = Mesh(
        mesh.devices.reshape(4, 12, 2, 2, mesh.shape["island"]),
        (*FSDP, ISLAND),
    )
    placed = (
        P(ISLAND, FSDP, None),
        P(ISLAND, FSDP, None),
        P(FSDP, None),
        P(ISLAND, None, None, None),
        P(ISLAND, None, None, None),
        P(ISLAND, FSDP, None),
        P(FSDP, None),
        P(FSDP, None),
    )
    return jax.shard_map(
        body,
        mesh=torus,
        in_specs=placed,
        out_specs=(
            P(FSDP, ISLAND),
            P(FSDP, None),
            P(ISLAND, None, None, None),
            P(ISLAND, None, None, None),
        ),
        check_vma=False,
    )
```

```python
import functools

import jax
import jax.numpy as jnp
from jax import lax
from jax.experimental import pallas as pl
from jax.experimental.pallas import tpu as pltpu
from jax.sharding import Mesh
from jax.sharding import PartitionSpec as P

RANK = 256
X, Z, Y, C = "fsdp_0", "fsdp_1", "fsdp_2", "fsdp_3"
ISLAND = "island"
FSDP = (X, Z, Y, C)
LANES = 128
RING_ORDER = (
    "iljkmpnoehfgababcdabehilfgcdabkjehgfmpcdabonehgf",
    "cdilqtrsahefmpuxvwdgtrcqshefuxwvgdqtsrehyzuxwvqt",
    "srxuwvqytzsrxuwvqtsryxuwvqtxu",
)
MESH_ID = pl.DeviceIdType.MESH
F32 = jnp.float32

first_decay = 0.9
second_decay = 0.999
first_fix = 1.0 - 0.9**10
second_fix = 1.0 - 0.999**10
epsilon = 1e-08
inner_rate = 1.0
outer_rate = 0.7
outer_beta = 0.9


class Lanes:
    def __init__(self, send_sems, recv_sems):
        self.send_sems, self.recv_sems = send_sems, recv_sems
        self.used = 0
        self.started = []

    def send(self, src, dst, **peer):
        copy = pltpu.make_async_remote_copy(
            src_ref=src,
            dst_ref=dst,
            send_sem=self.send_sems.at[self.used],
            recv_sem=self.recv_sems.at[self.used],
            device_id=peer,
            device_id_type=MESH_ID,
        )
        self.used += 1
        copy.start()
        self.started.append(copy)
        return copy


def turn(axis, by):
    size = lax.axis_size(axis)
    return lax.rem(lax.axis_index(axis) + by + size, size)


def chain(lanes, axis, steps, way, block, slots):
    copy = None
    for step in range(steps):
        at = block(turn(axis, way * (steps - step)))
        if copy is not None:
            copy.wait_recv()
            at[...] = at[...] + slots[step - 1]
        copy = lanes.send(at, slots.at[step], **{axis: turn(axis, way)})
        yield
    copy.wait_recv()
    at = block(lax.axis_index(axis))
    at[...] = at[...] + slots[steps - 1]


def advance(chains):
    for one in chains:
        next(one, None)


def comm_kernel(
    a_hbm, g_hbm, p_hbm, first_hbm, second_hbm, w_hbm,
    proj_ref, total_ref,
    a_ref, g_ref, p_ref, first_ref, second_ref,
    a_out, a_in, g_out, g_in, p_out, p_in, p_all,
    part_z, part_x,
    z_up, z_down, xa_up, xa_down, xb_up, xb_down,
    zx_up, zx_down, sa_up, sa_down, sb_up, sb_down,
    y_z, y_x, grad, grad_own, w_all, grad_all,
    proj_part, proj_x, proj_z, proj_all, stats, scale_all,
    send_sems, recv_sems, load_sems,
):
    xk, zk, yk, ck = (lax.axis_index(name) for name in FSDP)
    island = lax.axis_index(ISLAND)
    nx, nz = lax.axis_size(X), lax.axis_size(Z)
    ni = lax.axis_size(ISLAND)
    lanes = Lanes(send_sems, recv_sems)
    other_c, other_y = 1 - ck, 1 - yk
    quad = yk * 2 + ck
    half = g_ref.shape[1] // 2
    depth = first_ref.shape[0]
    rows = p_ref.shape[0]
    height = part_z.shape[2]
    mine = pl.ds(pl.multiple_of(ck * half, half), half)
    theirs = pl.ds(pl.multiple_of(other_c * half, half), half)
    here = pl.ds(pl.multiple_of((xk * 2 + yk) * depth, depth), depth)

    def near(by_x, by_y, by_c=0):
        peer = {}
        if by_x:
            peer[X] = turn(X, by_x)
        if by_y:
            peer[Y] = other_y
        if by_c:
            peer[C] = other_c
        return peer

    moves = [
        (g_hbm, g_ref), (a_hbm, a_ref), (p_hbm, p_ref),
        (w_hbm, w_all.at[island]),
        (first_hbm.at[here, mine], first_ref), (second_hbm.at[here, mine], second_ref),
    ]
    loads = [
        pltpu.make_async_copy(src, dst, load_sems.at[at])
        for at, (src, dst) in enumerate(moves)
    ]
    for load in loads:
        load.start()

    barrier = pltpu.get_barrier_semaphore()
    around = [
        near(i % nx, i // nx % 2, i // (2 * nx)) for i in range(1, 4 * nx)
    ]
    partners = around + [{Z: turn(Z, 1)}, {Z: turn(Z, -1)}]
    partners += [{ISLAND: turn(ISLAND, by)} for by in range(1, ni)]
    for partner in partners:
        pl.semaphore_signal(barrier, inc=1, device_id=partner, device_id_type=MESH_ID)
    loads[0].wait()
    g_out[...] = g_ref[:, theirs].astype(F32)
    loads[1].wait()
    a_out[...] = a_ref[...].astype(F32)
    loads[2].wait()
    p_out[...] = p_ref[...].astype(F32)
    pl.semaphore_wait(barrier, len(partners))

    wide = 11 * LANES
    spans = [slice(at, at + wide) for at in range(0, a_ref.shape[1], wide)]
    got_g = lanes.send(g_out, g_in, **{C: other_c})
    got_a = [lanes.send(a_out.at[:, at], a_in.at[:, at], **{C: other_c}) for at in spans]
    got_p = [
        lanes.send(p_out, p_in.at[quad], **near(0, y, c)) for y, c in ((0, 1), (1, 0), (1, 1))
    ]
    got_w = [
        lanes.send(w_hbm, w_all.at[island], **{ISLAND: turn(ISLAND, by)})
        for by in range(1, ni)
    ]

    def product(a, g, span, add):
        count = wide // height
        lhs = a[:, span].astype(jnp.bfloat16)
        out = lax.dot_general(lhs, g, (((0,), (0,)), ((), ())), preferred_element_type=F32)
        out = out.reshape(count, height, half)
        block = span.start // height
        done = 0
        while done < count:
            x, z = divmod(block + done, nz)
            take = min(nz - z, count - done)
            for ref, cols in ((part_z, slice(0, LANES)), (part_x, slice(LANES, half))):
                piece = out[done : done + take, :, cols]
                if add:
                    piece = ref[x, z : z + take] + piece
                ref[x, z : z + take] = piece
            done += take

    for span in spans:
        product(a_ref, g_ref[:, mine], span, False)
    p_in[quad] = p_out[...]

    up_z, up_x = nz // 2, nx // 2
    cut = xa_up.shape[3]
    both = ((1, 0), (-1, 1))
    chain_z, chain_a, chain_b = [], [], []
    for sub in range(nx):
        block = lambda d, sub=sub: part_z.at[sub, d]
        for way, slots in ((1, z_up), (-1, z_down)):
            less = int((way == 1) == (sub % 2 == 1))
            chain_z.append(chain(lanes, Z, up_z - less, way, block, slots.at[sub]))
    for chains, up, down, span in (
        (chain_a, xa_up, xa_down, slice(0, cut)),
        (chain_b, xb_up, xb_down, slice(cut, height)),
    ):
        for sub in range(2):
            lead = slice(sub * (nz // 2), (sub + 1) * (nz // 2))
            block = lambda d, lead=lead, span=span: part_x.at[d, lead, span]
            for way, slots in ((1, up), (-1, down)):
                less = int((way == 1) == (sub == 1))
                chains.append(chain(lanes, X, up_x - less, way, block, slots.at[sub]))
    block_z = lambda d: part_z.at[d, zk]
    last_x = []
    for start, stop, up, down in ((0, cut, sa_up, sa_down), (cut, height, sb_up, sb_down)):
        middle = start + -(-(stop - start) // 16) * 8
        for span in (slice(start, middle), slice(middle, stop)):
            less = len(last_x) // 2 % 2
            inner = slice(span.start - start, span.stop - start)
            block = lambda d, span=span: part_x.at[xk, d, span]
            last_x.append(chain(lanes, Z, up_z - less, 1, block, up.at[:, inner]))
            last_x.append(chain(lanes, Z, up_z - 1 + less, -1, block, down.at[:, inner]))
    last_z = [
        chain(lanes, X, up_x - less, way, block_z, slots)
        for (way, less), slots in zip(both, (zx_up, zx_down))
    ]
    got_g.wait_recv()
    ready = 0
    for copy, span in zip(got_a, spans):
        copy.wait_recv()
        product(a_in, g_in[...].astype(jnp.bfloat16), span, True)
        while ready < nx // 2 and (ready + 1) * nz * height <= span.stop:
            advance(chain_z[2 * ready : 2 * ready + 2])
            ready += 1
    every = chain_z + chain_a + chain_b + last_x + last_z
    for letter in "".join(RING_ORDER):
        at = ord(letter) - ord("a")
        advance([every[at]])
    for chains in (chain_z, chain_a, chain_b, last_x, last_z):
        for _ in range(up_z + 1):
            advance(chains)
    got_yz = lanes.send(part_z.at[xk, zk], y_z, **{Y: other_y})
    got_yx = lanes.send(part_x.at[xk, zk], y_x, **{Y: other_y})
    for copy in got_p:
        copy.wait_recv()
    for j in range(4):
        p_all[j * rows : (j + 1) * rows, :] = p_in[j]

    proj_part[...] = lax.dot_general(
        p_all[...],
        jnp.concatenate([part_z[xk, zk], part_x[xk, zk]], axis=1),
        (((0,), (0,)), ((), ())),
        precision=lax.Precision.HIGHEST,
        preferred_element_type=F32,
    ).reshape(proj_part.shape)
    got_x = []
    for i in range(1, 2 * nx):
        by_x, by_y = i % nx, i // nx
        to_x = turn(X, by_x)
        to_y = other_y if by_y else yk
        got_x.append(
            lanes.send(proj_part.at[to_x, to_y], proj_x.at[i - 1], **near(by_x, by_y))
        )

    got_yz.wait_recv()
    got_yx.wait_recv()
    grad[:, mine] = jnp.concatenate(
        [part_z[xk, zk] + y_z[...], part_x[xk, zk] + y_x[...]], axis=1
    )
    got_grad = lanes.send(grad.at[:, mine], grad.at[:, mine], **{C: other_c})
    own = proj_part[xk, yk]
    for i, copy in enumerate(got_x):
        copy.wait_recv()
        own = own + proj_x[i]
    proj_z[zk] = own

    pieces = [slice(at, at + 8) for at in range(0, depth, 8)]
    ups, downs = [None] * len(pieces), [None] * len(pieces)
    for step in range(up_z):
        for at, piece in enumerate(pieces):
            for way, held, last in ((1, ups, up_z), (-1, downs, up_z - 1)):
                if step >= last:
                    continue
                if step:
                    held[at].wait_recv()
                source = proj_z.at[turn(Z, -way * step), piece]
                held[at] = lanes.send(source, source, **{Z: turn(Z, way)})
        if step == min(2, up_z - 1):
            got_grad.wait_recv()
            for j in range(4):
                @pl.when(quad == j)
                def _(j=j):
                    grad_own[...] = grad[j * rows : (j + 1) * rows, :]
            got_gi = [
                lanes.send(grad_own, grad_all.at[island], **{ISLAND: turn(ISLAND, by)})
                for by in range(1, ni)
            ]
    grad_all[island] = grad_own[...]
    for load in loads[3:]:
        load.wait()
    for copy in ups + downs:
        copy.wait_recv()
    block = proj_z[0]
    for z in range(1, nz):
        block = block + proj_z[z]
    new_first = first_decay * first_ref[...] + (1.0 - first_decay) * block
    new_second = second_decay * second_ref[...] + (1.0 - second_decay) * block * block
    adapted = new_first / first_fix / (jnp.sqrt(new_second / second_fix) + epsilon)
    place = (ck * nx + xk) * 2 + yk
    stats[place, 0:1] = jnp.sum(adapted * adapted, axis=0, keepdims=True)
    stats[place, 1:2] = jnp.sum(block * block, axis=0, keepdims=True)
    got_stats = [lanes.send(stats.at[place], stats.at[place], **peer) for peer in around]
    proj_all[xk, yk, :, mine] = block
    got_proj = []
    for i in range(1, 2 * nx):
        spot = proj_all.at[xk, yk, :, mine]
        got_proj.append(lanes.send(spot, spot, **near(i % nx, i // nx)))
    for copy in got_stats:
        copy.wait_recv()
    for core in range(2):
        sums = stats[2 * nx * core]
        for i in range(1, 2 * nx):
            sums = sums + stats[2 * nx * core + i]
        sums = sums / RANK
        scale_all[island, :, core * half : (core + 1) * half] = jnp.sqrt(
            sums[0:1]
        ) / jnp.sqrt(sums[1:2] + 1e-06)
    got_si = [
        lanes.send(
            scale_all.at[island], scale_all.at[island], **{ISLAND: turn(ISLAND, by)}
        )
        for by in range(1, ni)
    ]

    for copy in got_proj:
        copy.wait_recv()
    spot = proj_all.at[:, :, :, mine]
    got_close = lanes.send(spot, spot, **{C: other_c})
    for copy in got_w + got_gi:
        copy.wait_recv()
    weights = w_all[0]
    for i in range(1, ni):
        weights = weights + w_all[i]
    weights = weights.reshape(rows, grad_own.shape[1])
    for copy in got_si:
        copy.wait_recv()
    moved = None
    for i in range(ni):
        step = inner_rate * grad_all[i] * scale_all[i]
        moved = step if moved is None else moved + step
    total_ref[...] = weights - moved
    got_close.wait_recv()
    proj_ref[...] = proj_all[...].reshape(proj_ref.shape)
    for copy in lanes.started:
        copy.wait_send()


def exchange(a, g, p, first, second, w):
    tokens, features = a.shape
    cols = g.shape[1]
    half = cols // 2
    rows = p.shape[0]
    nx, nz, ni = lax.axis_size(X), lax.axis_size(Z), lax.axis_size(ISLAND)
    quad = 4 * rows
    cut = quad // 16 * 8 + 8
    ups, upx = nz // 2, nx // 2
    vmem = lambda *shape: pltpu.VMEM(shape, F32)
    depth = RANK // nx // 2
    scratch = [
        pltpu.VMEM(a.shape, a.dtype), pltpu.VMEM(g.shape, g.dtype), pltpu.VMEM(p.shape, p.dtype),
        vmem(depth, half), vmem(depth, half),
        vmem(tokens, features), vmem(tokens, features),
        vmem(tokens, half), vmem(tokens, half),
        vmem(rows, RANK), vmem(4, rows, RANK), vmem(quad, RANK),
        vmem(nx, nz, quad, LANES), vmem(nx, nz, quad, LANES),
        vmem(nx, ups, quad, LANES), vmem(nx, ups, quad, LANES),
        vmem(2, upx, nz // 2, cut, LANES), vmem(2, upx, nz // 2, cut, LANES),
        vmem(2, upx, nz // 2, quad - cut, LANES), vmem(2, upx, nz // 2, quad - cut, LANES),
        vmem(upx, quad, LANES), vmem(upx, quad, LANES),
        vmem(ups, cut, LANES), vmem(ups, cut, LANES),
        vmem(ups, quad - cut, LANES), vmem(ups, quad - cut, LANES),
        vmem(quad, LANES), vmem(quad, LANES),
        vmem(quad, cols), vmem(rows, cols),
        vmem(ni, *w.shape), vmem(ni, rows, cols),
        vmem(nx, 2, depth, half), vmem(2 * nx - 1, depth, half), vmem(nz, depth, half),
        vmem(nx, 2, depth, cols), vmem(4 * nx, 2, half), vmem(ni, 1, cols),
        pltpu.SemaphoreType.DMA((200,)),
        pltpu.SemaphoreType.DMA((200,)),
        pltpu.SemaphoreType.DMA((6,)),
    ]
    return pl.pallas_call(
        comm_kernel,
        name="exchange",
        out_shape=(
            jax.ShapeDtypeStruct((RANK, cols), F32),
            jax.ShapeDtypeStruct((rows, cols), F32),
        ),
        in_specs=[pl.BlockSpec(memory_space=pltpu.HBM)] * 6,
        out_specs=(pl.BlockSpec(memory_space=pltpu.VMEM),) * 2,
        scratch_shapes=scratch,
        compiler_params=pltpu.CompilerParams(
            collective_id=0, has_side_effects=True, vmem_limit_bytes=40 << 20
        ),
    )(*(pltpu.with_memory_space_constraint(v, pltpu.HBM) for v in (a, g, p, first, second, w)))


def body(
    activations,
    out_grads,
    projection,
    first_moment,
    second_moment,
    inner_weights,
    global_weights,
    outer_momentum,
):
    projected, stepped_sum = exchange(
        activations[0],
        out_grads[0],
        projection,
        first_moment[0, 0],
        second_moment[0, 0],
        inner_weights.reshape(-1, 1, inner_weights.shape[2]),
    )
    new_first = first_decay * first_moment[0, 0] + (1.0 - first_decay) * projected
    new_second = (
        second_decay * second_moment[0, 0] + (1.0 - second_decay) * projected * projected
    )
    island_count = lax.axis_size(ISLAND)
    pseudo_grad = global_weights - stepped_sum / island_count
    new_momentum = outer_beta * outer_momentum + pseudo_grad
    weights_next = (
        global_weights - outer_rate * (pseudo_grad + outer_beta * new_momentum)
    ).astype(jnp.bfloat16)
    block_cols = global_weights.shape[1] // island_count
    weights_block = lax.dynamic_slice_in_dim(
        weights_next, lax.axis_index(ISLAND) * block_cols, block_cols, 1
    )
    return (weights_block, new_momentum, new_first[None, None], new_second[None, None])


def solution(mesh):
    torus = Mesh(
        mesh.devices.reshape(4, 12, 2, 2, mesh.shape["island"]),
        (*FSDP, ISLAND),
    )
    placed = (
        P(ISLAND, FSDP, None),
        P(ISLAND, FSDP, None),
        P(FSDP, None),
        P(ISLAND, None, None, None),
        P(ISLAND, None, None, None),
        P(ISLAND, FSDP, None),
        P(FSDP, None),
        P(FSDP, None),
    )
    return jax.shard_map(
        body,
        mesh=torus,
        in_specs=placed,
        out_specs=(
            P(FSDP, ISLAND),
            P(FSDP, None),
            P(ISLAND, None, None, None),
            P(ISLAND, None, None, None),
        ),
        check_vma=False,
    )
```

```python
import functools

import jax
import jax.numpy as jnp
from jax import lax
from jax.experimental import pallas as pl
from jax.experimental.pallas import tpu as pltpu
from jax.sharding import Mesh
from jax.sharding import PartitionSpec as P

RANK = 256
X, Z, Y, C = "fsdp_0", "fsdp_1", "fsdp_2", "fsdp_3"
ISLAND = "island"
FSDP = (X, Z, Y, C)
LANES = 128
RING_ORDER = (
    "iljkmpnoehfgababcdabehilfgcdabkjehgfmpcdabonehgf",
    "cdilqrahefmptsgdrcqhefstgdqrehuvstqrsutvqrstuqrs",
    "tqt",
)
MESH_ID = pl.DeviceIdType.MESH
F32 = jnp.float32

first_decay = 0.9
second_decay = 0.999
first_fix = 1.0 - 0.9**10
second_fix = 1.0 - 0.999**10
epsilon = 1e-08
inner_rate = 1.0
outer_rate = 0.7
outer_beta = 0.9


class Lanes:
    def __init__(self, send_sems, recv_sems):
        self.send_sems, self.recv_sems = send_sems, recv_sems
        self.used = 0
        self.started = []

    def send(self, src, dst, **peer):
        copy = pltpu.make_async_remote_copy(
            src_ref=src,
            dst_ref=dst,
            send_sem=self.send_sems.at[self.used],
            recv_sem=self.recv_sems.at[self.used],
            device_id=peer,
            device_id_type=MESH_ID,
        )
        self.used += 1
        copy.start()
        self.started.append(copy)
        return copy


def turn(axis, by):
    size = lax.axis_size(axis)
    return lax.rem(lax.axis_index(axis) + by + size, size)


def chain(lanes, axis, steps, way, block, slots):
    copy = None
    for step in range(steps):
        at = block(turn(axis, way * (steps - step)))
        if copy is not None:
            copy.wait_recv()
            at[...] = at[...] + slots[step - 1]
        copy = lanes.send(at, slots.at[step], **{axis: turn(axis, way)})
        yield
    copy.wait_recv()
    at = block(lax.axis_index(axis))
    at[...] = at[...] + slots[steps - 1]


def advance(chains):
    for one in chains:
        next(one, None)


def comm_kernel(
    a_hbm, g_hbm, p_hbm, first_hbm, second_hbm, w_hbm,
    proj_ref, total_ref,
    a_ref, g_ref, p_ref, first_ref, second_ref,
    a_out, a_in, g_out, g_in, p_out, p_in, p_all,
    part_z, part_x,
    z_up, z_down, xa_up, xa_down, xb_up, xb_down,
    zx_up, zx_down, sa_up, sa_down, sb_up, sb_down,
    y_z, y_x, grad, grad_own, w_all, grad_all,
    proj_part, proj_x, proj_z, proj_all, stats, scale_all,
    send_sems, recv_sems, load_sems,
):
    xk, zk, yk, ck = (lax.axis_index(name) for name in FSDP)
    island = lax.axis_index(ISLAND)
    nx, nz = lax.axis_size(X), lax.axis_size(Z)
    ni = lax.axis_size(ISLAND)
    lanes = Lanes(send_sems, recv_sems)
    other_c, other_y = 1 - ck, 1 - yk
    quad = yk * 2 + ck
    half = g_ref.shape[1] // 2
    depth = first_ref.shape[0]
    rows = p_ref.shape[0]
    height = part_z.shape[2]
    mine = pl.ds(pl.multiple_of(ck * half, half), half)
    theirs = pl.ds(pl.multiple_of(other_c * half, half), half)
    here = pl.ds(pl.multiple_of((xk * 2 + yk) * depth, depth), depth)

    def near(by_x, by_y, by_c=0):
        peer = {}
        if by_x:
            peer[X] = turn(X, by_x)
        if by_y:
            peer[Y] = other_y
        if by_c:
            peer[C] = other_c
        return peer

    moves = [
        (g_hbm, g_ref), (a_hbm, a_ref), (p_hbm, p_ref),
        (w_hbm, w_all.at[island]),
        (first_hbm.at[here, mine], first_ref), (second_hbm.at[here, mine], second_ref),
    ]
    loads = [
        pltpu.make_async_copy(src, dst, load_sems.at[at])
        for at, (src, dst) in enumerate(moves)
    ]
    for load in loads:
        load.start()

    barrier = pltpu.get_barrier_semaphore()
    around = [
        near(i % nx, i // nx % 2, i // (2 * nx)) for i in range(1, 4 * nx)
    ]
    partners = around + [{Z: turn(Z, 1)}, {Z: turn(Z, -1)}]
    partners += [{ISLAND: turn(ISLAND, by)} for by in range(1, ni)]
    for partner in partners:
        pl.semaphore_signal(barrier, inc=1, device_id=partner, device_id_type=MESH_ID)
    loads[0].wait()
    g_out[...] = g_ref[:, theirs].astype(F32)
    loads[1].wait()
    a_out[...] = a_ref[...].astype(F32)
    loads[2].wait()
    p_out[...] = p_ref[...].astype(F32)
    pl.semaphore_wait(barrier, len(partners))

    wide = 11 * LANES
    spans = [slice(at, at + wide) for at in range(0, a_ref.shape[1], wide)]
    got_g = lanes.send(g_out, g_in, **{C: other_c})
    got_a = [lanes.send(a_out.at[:, at], a_in.at[:, at], **{C: other_c}) for at in spans]
    got_p = [
        lanes.send(p_out, p_in.at[quad], **near(0, y, c)) for y, c in ((0, 1), (1, 0), (1, 1))
    ]
    got_w = [
        lanes.send(w_hbm, w_all.at[island], **{ISLAND: turn(ISLAND, by)})
        for by in range(1, ni)
    ]

    def product(a, g, span, add):
        count = wide // height
        lhs = a[:, span].astype(jnp.bfloat16)
        out = lax.dot_general(lhs, g, (((0,), (0,)), ((), ())), preferred_element_type=F32)
        out = out.reshape(count, height, half)
        block = span.start // height
        done = 0
        while done < count:
            x, z = divmod(block + done, nz)
            take = min(nz - z, count - done)
            for ref, cols in ((part_z, slice(0, LANES)), (part_x, slice(LANES, half))):
                piece = out[done : done + take, :, cols]
                if add:
                    piece = ref[x, z : z + take] + piece
                ref[x, z : z + take] = piece
            done += take

    for span in spans:
        product(a_ref, g_ref[:, mine], span, False)
    p_in[quad] = p_out[...]

    up_z, up_x = nz // 2, nx // 2
    cut = xa_up.shape[3]
    both = ((1, 0), (-1, 1))
    chain_z, chain_a, chain_b = [], [], []
    for sub in range(nx):
        block = lambda d, sub=sub: part_z.at[sub, d]
        for way, slots in ((1, z_up), (-1, z_down)):
            less = int((way == 1) == (sub % 2 == 1))
            chain_z.append(chain(lanes, Z, up_z - less, way, block, slots.at[sub]))
    for chains, up, down, span in (
        (chain_a, xa_up, xa_down, slice(0, cut)),
        (chain_b, xb_up, xb_down, slice(cut, height)),
    ):
        for sub in range(2):
            lead = slice(sub * (nz // 2), (sub + 1) * (nz // 2))
            block = lambda d, lead=lead, span=span: part_x.at[d, lead, span]
            for way, slots in ((1, up), (-1, down)):
                less = int((way == 1) == (sub == 1))
                chains.append(chain(lanes, X, up_x - less, way, block, slots.at[sub]))
    block_a = lambda d: part_x.at[xk, d, slice(0, cut)]
    block_b = lambda d: part_x.at[xk, d, slice(cut, height)]
    block_z = lambda d: part_z.at[d, zk]
    last_a = [
        chain(lanes, Z, up_z - less, way, block_a, slots)
        for (way, less), slots in zip(both, (sa_up, sa_down))
    ]
    last_b = [
        chain(lanes, Z, up_z - 1 + less, way, block_b, slots)
        for (way, less), slots in zip(both, (sb_up, sb_down))
    ]
    last_z = [
        chain(lanes, X, up_x - less, way, block_z, slots)
        for (way, less), slots in zip(both, (zx_up, zx_down))
    ]
    got_g.wait_recv()
    ready = 0
    for copy, span in zip(got_a, spans):
        copy.wait_recv()
        product(a_in, g_in[...].astype(jnp.bfloat16), span, True)
        while ready < nx // 2 and (ready + 1) * nz * height <= span.stop:
            advance(chain_z[2 * ready : 2 * ready + 2])
            ready += 1
    every = chain_z + chain_a + chain_b + last_a + last_b + last_z
    for letter in "".join(RING_ORDER):
        at = ord(letter) - ord("a")
        advance([every[at]])
    for chains in (chain_z, chain_a, chain_b, last_a, last_b, last_z):
        for _ in range(up_z + 1):
            advance(chains)
    got_yz = lanes.send(part_z.at[xk, zk], y_z, **{Y: other_y})
    got_yx = lanes.send(part_x.at[xk, zk], y_x, **{Y: other_y})
    for copy in got_p:
        copy.wait_recv()
    for j in range(4):
        p_all[j * rows : (j + 1) * rows, :] = p_in[j]

    rest = jnp.concatenate([part_z[xk, zk], part_x[xk, zk]], axis=1)
    sides = p_all[...].astype(jnp.bfloat16)
    terms = None
    for _ in range(3):
        term = rest.astype(jnp.bfloat16)
        rest = rest - term.astype(F32)
        term = lax.dot_general(
            sides, term, (((0,), (0,)), ((), ())), preferred_element_type=F32
        )
        terms = term if terms is None else terms + term
    proj_part[...] = terms.reshape(proj_part.shape)
    got_x = []
    for i in range(1, 2 * nx):
        by_x, by_y = i % nx, i // nx
        to_x = turn(X, by_x)
        to_y = other_y if by_y else yk
        got_x.append(
            lanes.send(proj_part.at[to_x, to_y], proj_x.at[i - 1], **near(by_x, by_y))
        )

    got_yz.wait_recv()
    got_yx.wait_recv()
    grad[:, mine] = jnp.concatenate(
        [part_z[xk, zk] + y_z[...], part_x[xk, zk] + y_x[...]], axis=1
    )
    got_grad = lanes.send(grad.at[:, mine], grad.at[:, mine], **{C: other_c})
    own = proj_part[xk, yk]
    for i, copy in enumerate(got_x):
        copy.wait_recv()
        own = own + proj_x[i]
    proj_z[zk] = own

    ups, downs = [], []
    for step in range(up_z):
        for way, held, last in ((1, ups, up_z), (-1, downs, up_z - 1)):
            if step >= last:
                continue
            if held:
                held[-1].wait_recv()
            source = proj_z.at[turn(Z, -way * step)]
            held.append(lanes.send(source, source, **{Z: turn(Z, way)}))
        if step == min(2, up_z - 1):
            got_grad.wait_recv()
            for j in range(4):
                @pl.when(quad == j)
                def _(j=j):
                    grad_own[...] = grad[j * rows : (j + 1) * rows, :]
            got_gi = [
                lanes.send(grad_own, grad_all.at[island], **{ISLAND: turn(ISLAND, by)})
                for by in range(1, ni)
            ]
    grad_all[island] = grad_own[...]
    for load in loads[3:]:
        load.wait()
    ups[-1].wait_recv()
    downs[-1].wait_recv()
    block = proj_z[0]
    for z in range(1, nz):
        block = block + proj_z[z]
    new_first = first_decay * first_ref[...] + (1.0 - first_decay) * block
    new_second = second_decay * second_ref[...] + (1.0 - second_decay) * block * block
    adapted = new_first / first_fix / (jnp.sqrt(new_second / second_fix) + epsilon)
    place = (ck * nx + xk) * 2 + yk
    stats[place, 0:1] = jnp.sum(adapted * adapted, axis=0, keepdims=True)
    stats[place, 1:2] = jnp.sum(block * block, axis=0, keepdims=True)
    got_stats = [lanes.send(stats.at[place], stats.at[place], **peer) for peer in around]
    proj_all[xk, yk, :, mine] = block
    got_proj = []
    for i in range(1, 2 * nx):
        spot = proj_all.at[xk, yk, :, mine]
        got_proj.append(lanes.send(spot, spot, **near(i % nx, i // nx)))
    for copy in got_stats:
        copy.wait_recv()
    for core in range(2):
        sums = stats[2 * nx * core]
        for i in range(1, 2 * nx):
            sums = sums + stats[2 * nx * core + i]
        sums = sums / RANK
        scale_all[island, :, core * half : (core + 1) * half] = jnp.sqrt(
            sums[0:1]
        ) / jnp.sqrt(sums[1:2] + 1e-06)
    got_si = [
        lanes.send(
            scale_all.at[island], scale_all.at[island], **{ISLAND: turn(ISLAND, by)}
        )
        for by in range(1, ni)
    ]

    for copy in got_proj:
        copy.wait_recv()
    spot = proj_all.at[:, :, :, mine]
    got_close = lanes.send(spot, spot, **{C: other_c})
    for copy in got_w + got_gi:
        copy.wait_recv()
    weights = w_all[0]
    for i in range(1, ni):
        weights = weights + w_all[i]
    weights = weights.reshape(rows, grad_own.shape[1])
    for copy in got_si:
        copy.wait_recv()
    moved = None
    for i in range(ni):
        step = inner_rate * grad_all[i] * scale_all[i]
        moved = step if moved is None else moved + step
    total_ref[...] = weights - moved
    got_close.wait_recv()
    proj_ref[...] = proj_all[...].reshape(proj_ref.shape)
    for copy in lanes.started:
        copy.wait_send()


def exchange(a, g, p, first, second, w):
    tokens, features = a.shape
    cols = g.shape[1]
    half = cols // 2
    rows = p.shape[0]
    nx, nz, ni = lax.axis_size(X), lax.axis_size(Z), lax.axis_size(ISLAND)
    quad = 4 * rows
    cut = quad // 16 * 8 + 8
    ups, upx = nz // 2, nx // 2
    vmem = lambda *shape: pltpu.VMEM(shape, F32)
    depth = RANK // nx // 2
    scratch = [
        pltpu.VMEM(a.shape, a.dtype), pltpu.VMEM(g.shape, g.dtype), pltpu.VMEM(p.shape, p.dtype),
        vmem(depth, half), vmem(depth, half),
        vmem(tokens, features), vmem(tokens, features),
        vmem(tokens, half), vmem(tokens, half),
        vmem(rows, RANK), vmem(4, rows, RANK), vmem(quad, RANK),
        vmem(nx, nz, quad, LANES), vmem(nx, nz, quad, LANES),
        vmem(nx, ups, quad, LANES), vmem(nx, ups, quad, LANES),
        vmem(2, upx, nz // 2, cut, LANES), vmem(2, upx, nz // 2, cut, LANES),
        vmem(2, upx, nz // 2, quad - cut, LANES), vmem(2, upx, nz // 2, quad - cut, LANES),
        vmem(upx, quad, LANES), vmem(upx, quad, LANES),
        vmem(ups, cut, LANES), vmem(ups, cut, LANES),
        vmem(ups, quad - cut, LANES), vmem(ups, quad - cut, LANES),
        vmem(quad, LANES), vmem(quad, LANES),
        vmem(quad, cols), vmem(rows, cols),
        vmem(ni, *w.shape), vmem(ni, rows, cols),
        vmem(nx, 2, depth, half), vmem(2 * nx - 1, depth, half), vmem(nz, depth, half),
        vmem(nx, 2, depth, cols), vmem(4 * nx, 2, half), vmem(ni, 1, cols),
        pltpu.SemaphoreType.DMA((150,)),
        pltpu.SemaphoreType.DMA((150,)),
        pltpu.SemaphoreType.DMA((6,)),
    ]
    return pl.pallas_call(
        comm_kernel,
        name="exchange",
        out_shape=(
            jax.ShapeDtypeStruct((RANK, cols), F32),
            jax.ShapeDtypeStruct((rows, cols), F32),
        ),
        in_specs=[pl.BlockSpec(memory_space=pltpu.HBM)] * 6,
        out_specs=(pl.BlockSpec(memory_space=pltpu.VMEM),) * 2,
        scratch_shapes=scratch,
        compiler_params=pltpu.CompilerParams(
            collective_id=0, has_side_effects=True, vmem_limit_bytes=40 << 20
        ),
    )(*(pltpu.with_memory_space_constraint(v, pltpu.HBM) for v in (a, g, p, first, second, w)))


def body(
    activations,
    out_grads,
    projection,
    first_moment,
    second_moment,
    inner_weights,
    global_weights,
    outer_momentum,
):
    projected, stepped_sum = exchange(
        activations[0],
        out_grads[0],
        projection,
        first_moment[0, 0],
        second_moment[0, 0],
        inner_weights.reshape(-1, 1, inner_weights.shape[2]),
    )
    new_first = first_decay * first_moment[0, 0] + (1.0 - first_decay) * projected
    new_second = (
        second_decay * second_moment[0, 0] + (1.0 - second_decay) * projected * projected
    )
    island_count = lax.axis_size(ISLAND)
    pseudo_grad = global_weights - stepped_sum / island_count
    new_momentum = outer_beta * outer_momentum + pseudo_grad
    weights_next = (
        global_weights - outer_rate * (pseudo_grad + outer_beta * new_momentum)
    ).astype(jnp.bfloat16)
    block_cols = global_weights.shape[1] // island_count
    weights_block = lax.dynamic_slice_in_dim(
        weights_next, lax.axis_index(ISLAND) * block_cols, block_cols, 1
    )
    return (weights_block, new_momentum, new_first[None, None], new_second[None, None])


def solution(mesh):
    torus = Mesh(
        mesh.devices.reshape(4, 12, 2, 2, mesh.shape["island"]),
        (*FSDP, ISLAND),
    )
    placed = (
        P(ISLAND, FSDP, None),
        P(ISLAND, FSDP, None),
        P(FSDP, None),
        P(ISLAND, None, None, None),
        P(ISLAND, None, None, None),
        P(ISLAND, FSDP, None),
        P(FSDP, None),
        P(FSDP, None),
    )
    return jax.shard_map(
        body,
        mesh=torus,
        in_specs=placed,
        out_specs=(
            P(FSDP, ISLAND),
            P(FSDP, None),
            P(ISLAND, None, None, None),
            P(ISLAND, None, None, None),
        ),
        check_vma=False,
    )
```

```python
import functools

import jax
import jax.numpy as jnp
from jax import lax
from jax.experimental import pallas as pl
from jax.experimental.pallas import tpu as pltpu
from jax.sharding import Mesh
from jax.sharding import PartitionSpec as P

RANK = 256
X, Z, Y, C = "fsdp_0", "fsdp_1", "fsdp_2", "fsdp_3"
ISLAND = "island"
FSDP = (X, Z, Y, C)
LANES = 128
RING_ORDER = (
    "iljkmpnoehfgadehilbcgfajkdehcbmpgfadonehcbgilqrf",
    "adehmptscbrgqfadehstcbrgqfadehuvstqrstuvqrstqrus",
    "tqt",
)
MESH_ID = pl.DeviceIdType.MESH
F32 = jnp.float32

first_decay = 0.9
second_decay = 0.999
first_fix = 1.0 - 0.9**10
second_fix = 1.0 - 0.999**10
epsilon = 1e-08
inner_rate = 1.0
outer_rate = 0.7
outer_beta = 0.9


class Lanes:
    def __init__(self, send_sems, recv_sems):
        self.send_sems, self.recv_sems = send_sems, recv_sems
        self.used = 0
        self.started = []

    def send(self, src, dst, **peer):
        copy = pltpu.make_async_remote_copy(
            src_ref=src,
            dst_ref=dst,
            send_sem=self.send_sems.at[self.used],
            recv_sem=self.recv_sems.at[self.used],
            device_id=peer,
            device_id_type=MESH_ID,
        )
        self.used += 1
        copy.start()
        self.started.append(copy)
        return copy


def turn(axis, by):
    size = lax.axis_size(axis)
    return lax.rem(lax.axis_index(axis) + by + size, size)


def chain(lanes, axis, steps, way, block, slots):
    copy = None
    for step in range(steps):
        at = block(turn(axis, way * (steps - step)))
        if copy is not None:
            copy.wait_recv()
            at[...] = at[...] + slots[step - 1]
        copy = lanes.send(at, slots.at[step], **{axis: turn(axis, way)})
        yield
    copy.wait_recv()
    at = block(lax.axis_index(axis))
    at[...] = at[...] + slots[steps - 1]


def advance(chains):
    for one in chains:
        next(one, None)


def comm_kernel(
    a_hbm, g_hbm, p_hbm, first_hbm, second_hbm, w_hbm,
    proj_ref, total_ref,
    a_ref, g_ref, p_ref, first_ref, second_ref,
    a_out, a_in, g_out, g_in, p_out, p_in, p_all,
    part_z, part_x,
    z_up, z_down, xa_up, xa_down, xb_up, xb_down,
    zx_up, zx_down, sa_up, sa_down, sb_up, sb_down,
    y_z, y_x, grad, grad_own, w_all, grad_all,
    proj_part, proj_x, proj_z, proj_all, stats, scale_all,
    send_sems, recv_sems, load_sems,
):
    xk, zk, yk, ck = (lax.axis_index(name) for name in FSDP)
    island = lax.axis_index(ISLAND)
    nx, nz = lax.axis_size(X), lax.axis_size(Z)
    ni = lax.axis_size(ISLAND)
    lanes = Lanes(send_sems, recv_sems)
    other_c, other_y = 1 - ck, 1 - yk
    quad = yk * 2 + ck
    half = g_ref.shape[1] // 2
    depth = first_ref.shape[0]
    rows = p_ref.shape[0]
    height = part_z.shape[2]
    mine = pl.ds(pl.multiple_of(ck * half, half), half)
    theirs = pl.ds(pl.multiple_of(other_c * half, half), half)
    here = pl.ds(pl.multiple_of((xk * 2 + yk) * depth, depth), depth)

    def near(by_x, by_y, by_c=0):
        peer = {}
        if by_x:
            peer[X] = turn(X, by_x)
        if by_y:
            peer[Y] = other_y
        if by_c:
            peer[C] = other_c
        return peer

    moves = [
        (g_hbm, g_ref), (a_hbm, a_ref), (p_hbm, p_ref),
        (w_hbm, w_all.at[island]),
        (first_hbm.at[here, mine], first_ref), (second_hbm.at[here, mine], second_ref),
    ]
    loads = [
        pltpu.make_async_copy(src, dst, load_sems.at[at])
        for at, (src, dst) in enumerate(moves)
    ]
    for load in loads:
        load.start()

    barrier = pltpu.get_barrier_semaphore()
    around = [
        near(i % nx, i // nx % 2, i // (2 * nx)) for i in range(1, 4 * nx)
    ]
    partners = around + [{Z: turn(Z, 1)}, {Z: turn(Z, -1)}]
    partners += [{ISLAND: turn(ISLAND, by)} for by in range(1, ni)]
    for partner in partners:
        pl.semaphore_signal(barrier, inc=1, device_id=partner, device_id_type=MESH_ID)
    loads[0].wait()
    g_out[...] = g_ref[:, theirs].astype(F32)
    loads[1].wait()
    a_out[...] = a_ref[...].astype(F32)
    loads[2].wait()
    p_out[...] = p_ref[...].astype(F32)
    pl.semaphore_wait(barrier, len(partners))

    wide = 11 * LANES
    spans = [slice(at, at + wide) for at in range(0, a_ref.shape[1], wide)]
    got_g = lanes.send(g_out, g_in, **{C: other_c})
    got_a = [lanes.send(a_out.at[:, at], a_in.at[:, at], **{C: other_c}) for at in spans]
    got_p = [
        lanes.send(p_out, p_in.at[quad], **near(0, y, c)) for y, c in ((0, 1), (1, 0), (1, 1))
    ]
    got_w = [
        lanes.send(w_hbm, w_all.at[island], **{ISLAND: turn(ISLAND, by)})
        for by in range(1, ni)
    ]

    def product(a, g, span, add):
        count = wide // height
        lhs = a[:, span].astype(jnp.bfloat16)
        out = lax.dot_general(lhs, g, (((0,), (0,)), ((), ())), preferred_element_type=F32)
        out = out.reshape(count, height, half)
        block = span.start // height
        done = 0
        while done < count:
            x, z = divmod(block + done, nz)
            take = min(nz - z, count - done)
            for ref, cols in ((part_z, slice(0, LANES)), (part_x, slice(LANES, half))):
                piece = out[done : done + take, :, cols]
                if add:
                    piece = ref[x, z : z + take] + piece
                ref[x, z : z + take] = piece
            done += take

    for span in spans:
        product(a_ref, g_ref[:, mine], span, False)
    p_in[quad] = p_out[...]

    up_z, up_x = nz // 2, nx // 2
    cut = xa_up.shape[3]
    both = ((1, 0), (-1, 1))
    chain_z, chain_a, chain_b = [], [], []
    for sub in range(nx):
        block = lambda d, sub=sub: part_z.at[sub, d]
        for way, slots in ((1, z_up), (-1, z_down)):
            less = int((way == 1) == (sub % 2 == 1))
            chain_z.append(chain(lanes, Z, up_z - less, way, block, slots.at[sub]))
    for chains, up, down, span in (
        (chain_a, xa_up, xa_down, slice(0, cut)),
        (chain_b, xb_up, xb_down, slice(cut, height)),
    ):
        for sub in range(2):
            lead = slice(sub * (nz // 2), (sub + 1) * (nz // 2))
            block = lambda d, lead=lead, span=span: part_x.at[d, lead, span]
            for way, slots in ((1, up), (-1, down)):
                less = int((way == 1) == (sub == 1))
                chains.append(chain(lanes, X, up_x - less, way, block, slots.at[sub]))
    block_a = lambda d: part_x.at[xk, d, slice(0, cut)]
    block_b = lambda d: part_x.at[xk, d, slice(cut, height)]
    block_z = lambda d: part_z.at[d, zk]
    last_a = [
        chain(lanes, Z, up_z - less, way, block_a, slots)
        for (way, less), slots in zip(both, (sa_up, sa_down))
    ]
    last_b = [
        chain(lanes, Z, up_z - 1 + less, way, block_b, slots)
        for (way, less), slots in zip(both, (sb_up, sb_down))
    ]
    last_z = [
        chain(lanes, X, up_x - less, way, block_z, slots)
        for (way, less), slots in zip(both, (zx_up, zx_down))
    ]
    got_g.wait_recv()
    ready = 0
    for copy, span in zip(got_a, spans):
        copy.wait_recv()
        product(a_in, g_in[...].astype(jnp.bfloat16), span, True)
        while ready < nx // 2 and (ready + 1) * nz * height <= span.stop:
            advance(chain_z[2 * ready : 2 * ready + 2])
            ready += 1
    every = chain_z + chain_a + chain_b + last_a + last_b + last_z
    for letter in "".join(RING_ORDER):
        at = ord(letter) - ord("a")
        advance([every[at]])
    for chains in (chain_z, chain_a, chain_b, last_a, last_b, last_z):
        for _ in range(up_z + 1):
            advance(chains)
    got_yz = lanes.send(part_z.at[xk, zk], y_z, **{Y: other_y})
    got_yx = lanes.send(part_x.at[xk, zk], y_x, **{Y: other_y})
    for copy in got_p:
        copy.wait_recv()
    for j in range(4):
        p_all[j * rows : (j + 1) * rows, :] = p_in[j]

    rest = jnp.concatenate([part_z[xk, zk], part_x[xk, zk]], axis=1)
    sides = p_all[...].astype(jnp.bfloat16)
    terms = None
    for _ in range(3):
        term = rest.astype(jnp.bfloat16)
        rest = rest - term.astype(F32)
        term = lax.dot_general(
            sides, term, (((0,), (0,)), ((), ())), preferred_element_type=F32
        )
        terms = term if terms is None else terms + term
    proj_part[...] = terms.reshape(proj_part.shape)
    got_x = []
    for i in range(1, 2 * nx):
        by_x, by_y = i % nx, i // nx
        to_x = turn(X, by_x)
        to_y = other_y if by_y else yk
        got_x.append(
            lanes.send(proj_part.at[to_x, to_y], proj_x.at[i - 1], **near(by_x, by_y))
        )

    got_yz.wait_recv()
    got_yx.wait_recv()
    grad[:, mine] = jnp.concatenate(
        [part_z[xk, zk] + y_z[...], part_x[xk, zk] + y_x[...]], axis=1
    )
    got_grad = lanes.send(grad.at[:, mine], grad.at[:, mine], **{C: other_c})
    own = proj_part[xk, yk]
    for i, copy in enumerate(got_x):
        copy.wait_recv()
        own = own + proj_x[i]
    proj_z[zk] = own

    ups, downs = [], []
    for step in range(up_z):
        for way, held, last in ((1, ups, up_z), (-1, downs, up_z - 1)):
            if step >= last:
                continue
            if held:
                held[-1].wait_recv()
            source = proj_z.at[turn(Z, -way * step)]
            held.append(lanes.send(source, source, **{Z: turn(Z, way)}))
        if step == min(2, up_z - 1):
            got_grad.wait_recv()
            for j in range(4):
                @pl.when(quad == j)
                def _(j=j):
                    grad_own[...] = grad[j * rows : (j + 1) * rows, :]
            got_gi = [
                lanes.send(grad_own, grad_all.at[island], **{ISLAND: turn(ISLAND, by)})
                for by in range(1, ni)
            ]
    grad_all[island] = grad_own[...]
    for load in loads[3:]:
        load.wait()
    ups[-1].wait_recv()
    downs[-1].wait_recv()
    block = proj_z[0]
    for z in range(1, nz):
        block = block + proj_z[z]
    new_first = first_decay * first_ref[...] + (1.0 - first_decay) * block
    new_second = second_decay * second_ref[...] + (1.0 - second_decay) * block * block
    adapted = new_first / first_fix / (jnp.sqrt(new_second / second_fix) + epsilon)
    place = (ck * nx + xk) * 2 + yk
    stats[place, 0:1] = jnp.sum(adapted * adapted, axis=0, keepdims=True)
    stats[place, 1:2] = jnp.sum(block * block, axis=0, keepdims=True)
    got_stats = [lanes.send(stats.at[place], stats.at[place], **peer) for peer in around]
    proj_all[xk, yk, :, mine] = block
    got_proj = []
    for i in range(1, 2 * nx):
        spot = proj_all.at[xk, yk, :, mine]
        got_proj.append(lanes.send(spot, spot, **near(i % nx, i // nx)))
    for copy in got_stats:
        copy.wait_recv()
    for core in range(2):
        sums = stats[2 * nx * core]
        for i in range(1, 2 * nx):
            sums = sums + stats[2 * nx * core + i]
        sums = sums / RANK
        scale_all[island, :, core * half : (core + 1) * half] = jnp.sqrt(
            sums[0:1]
        ) / jnp.sqrt(sums[1:2] + 1e-06)
    got_si = [
        lanes.send(
            scale_all.at[island], scale_all.at[island], **{ISLAND: turn(ISLAND, by)}
        )
        for by in range(1, ni)
    ]

    for copy in got_proj:
        copy.wait_recv()
    spot = proj_all.at[:, :, :, mine]
    got_close = lanes.send(spot, spot, **{C: other_c})
    for copy in got_w + got_gi:
        copy.wait_recv()
    weights = w_all[0]
    for i in range(1, ni):
        weights = weights + w_all[i]
    weights = weights.reshape(rows, grad_own.shape[1])
    for copy in got_si:
        copy.wait_recv()
    moved = None
    for i in range(ni):
        step = inner_rate * grad_all[i] * scale_all[i]
        moved = step if moved is None else moved + step
    total_ref[...] = weights - moved
    got_close.wait_recv()
    proj_ref[...] = proj_all[...].reshape(proj_ref.shape)
    for copy in lanes.started:
        copy.wait_send()


def exchange(a, g, p, first, second, w):
    tokens, features = a.shape
    cols = g.shape[1]
    half = cols // 2
    rows = p.shape[0]
    nx, nz, ni = lax.axis_size(X), lax.axis_size(Z), lax.axis_size(ISLAND)
    quad = 4 * rows
    cut = quad // 16 * 8 + 8
    ups, upx = nz // 2, nx // 2
    vmem = lambda *shape: pltpu.VMEM(shape, F32)
    depth = RANK // nx // 2
    scratch = [
        pltpu.VMEM(a.shape, a.dtype), pltpu.VMEM(g.shape, g.dtype), pltpu.VMEM(p.shape, p.dtype),
        vmem(depth, half), vmem(depth, half),
        vmem(tokens, features), vmem(tokens, features),
        vmem(tokens, half), vmem(tokens, half),
        vmem(rows, RANK), vmem(4, rows, RANK), vmem(quad, RANK),
        vmem(nx, nz, quad, LANES), vmem(nx, nz, quad, LANES),
        vmem(nx, ups, quad, LANES), vmem(nx, ups, quad, LANES),
        vmem(2, upx, nz // 2, cut, LANES), vmem(2, upx, nz // 2, cut, LANES),
        vmem(2, upx, nz // 2, quad - cut, LANES), vmem(2, upx, nz // 2, quad - cut, LANES),
        vmem(upx, quad, LANES), vmem(upx, quad, LANES),
        vmem(ups, cut, LANES), vmem(ups, cut, LANES),
        vmem(ups, quad - cut, LANES), vmem(ups, quad - cut, LANES),
        vmem(quad, LANES), vmem(quad, LANES),
        vmem(quad, cols), vmem(rows, cols),
        vmem(ni, *w.shape), vmem(ni, rows, cols),
        vmem(nx, 2, depth, half), vmem(2 * nx - 1, depth, half), vmem(nz, depth, half),
        vmem(nx, 2, depth, cols), vmem(4 * nx, 2, half), vmem(ni, 1, cols),
        pltpu.SemaphoreType.DMA((150,)),
        pltpu.SemaphoreType.DMA((150,)),
        pltpu.SemaphoreType.DMA((6,)),
    ]
    return pl.pallas_call(
        comm_kernel,
        name="exchange",
        out_shape=(
            jax.ShapeDtypeStruct((RANK, cols), F32),
            jax.ShapeDtypeStruct((rows, cols), F32),
        ),
        in_specs=[pl.BlockSpec(memory_space=pltpu.HBM)] * 6,
        out_specs=(pl.BlockSpec(memory_space=pltpu.VMEM),) * 2,
        scratch_shapes=scratch,
        compiler_params=pltpu.CompilerParams(
            collective_id=0, has_side_effects=True, vmem_limit_bytes=40 << 20
        ),
    )(*(pltpu.with_memory_space_constraint(v, pltpu.HBM) for v in (a, g, p, first, second, w)))


def body(
    activations,
    out_grads,
    projection,
    first_moment,
    second_moment,
    inner_weights,
    global_weights,
    outer_momentum,
):
    projected, stepped_sum = exchange(
        activations[0],
        out_grads[0],
        projection,
        first_moment[0, 0],
        second_moment[0, 0],
        inner_weights.reshape(-1, 1, inner_weights.shape[2]),
    )
    new_first = first_decay * first_moment[0, 0] + (1.0 - first_decay) * projected
    new_second = (
        second_decay * second_moment[0, 0] + (1.0 - second_decay) * projected * projected
    )
    island_count = lax.axis_size(ISLAND)
    pseudo_grad = global_weights - stepped_sum / island_count
    new_momentum = outer_beta * outer_momentum + pseudo_grad
    weights_next = (
        global_weights - outer_rate * (pseudo_grad + outer_beta * new_momentum)
    ).astype(jnp.bfloat16)
    block_cols = global_weights.shape[1] // island_count
    weights_block = lax.dynamic_slice_in_dim(
        weights_next, lax.axis_index(ISLAND) * block_cols, block_cols, 1
    )
    return (weights_block, new_momentum, new_first[None, None], new_second[None, None])


def solution(mesh):
    torus = Mesh(
        mesh.devices.reshape(4, 12, 2, 2, mesh.shape["island"]),
        (*FSDP, ISLAND),
    )
    placed = (
        P(ISLAND, FSDP, None),
        P(ISLAND, FSDP, None),
        P(FSDP, None),
        P(ISLAND, None, None, None),
        P(ISLAND, None, None, None),
        P(ISLAND, FSDP, None),
        P(FSDP, None),
        P(FSDP, None),
    )
    return jax.shard_map(
        body,
        mesh=torus,
        in_specs=placed,
        out_specs=(
            P(FSDP, ISLAND),
            P(FSDP, None),
            P(ISLAND, None, None, None),
            P(ISLAND, None, None, None),
        ),
        check_vma=False,
    )
```
